32 devices in a mesh: sub: 4 (over x, core), blk: 8 (over z, y).
Axes of the slice: x: 2, y: 2, z: 4, core: 2. Of those that a mesh axis runs over, the one named last changes fastest.
Arguments:
- root_inverse: bfloat16 [8192, 8192], P('blk', 'sub'), as said below
- factor_panel: bfloat16 [8192, 2048], P('blk', 'sub'), may hold values from -0.09375 to 0.09375
- diag_inverse: bfloat16 [512, 2048], P('blk', 'sub'), as said below
- pattern: int32 [4, 16], P('sub'), may hold values 0 or 1
Outputs:
- cross_block: bfloat16 [8192, 2048], P('blk', 'sub')
- diag_block: float32 [512, 2048], P('blk', 'sub')
The draws below stay inside these ranges and needn't reach their ends.
Inputs may be any that keep to these rules, and one draw needn't show every extreme that they name: `root_inverse`: symmetric. `diag_inverse`: each group's 512 x 512 block is lower triangular.
All inputs are finite; a program needn't handle non-finite values. No bound on the sum of `pattern` on one device may be relied on, other than what follows from the above.
Results may differ from the reference program's by a relative error of at most 0.0085.
Values may be sent and summed in bfloat16 or wider, within the bound.
A program may use at most 128 MiB of HBM per device.

```python
import jax
import jax.numpy as jnp

BLOCK = 512
ROOT = 8192
ROOT_BLOCKS = 16
PANEL = 512
GROUPS = 4


def draw_root_inverse(key, part):
    first, second = jax.random.split(key)
    noise = jax.random.normal(first, (ROOT, ROOT), jnp.float32)
    spread = 3.0 * (noise + noise.T) / jnp.sqrt(2.0 * ROOT)
    levels = jax.random.uniform(second, (ROOT,), jnp.float32, 4.0, 8.0)
    identity = (jnp.arange(ROOT)[:, None] == jnp.arange(ROOT)[None, :]).astype(jnp.float32)
    return (spread + identity * levels[:, None]).astype(jnp.bfloat16)


def draw_diag_inverse(key, part):
    first, second = jax.random.split(key)
    noise = jax.random.normal(first, (PANEL, GROUPS, PANEL), jnp.float32)
    rows_at = jnp.arange(PANEL)[:, None, None]
    cols_at = jnp.arange(PANEL)[None, None, :]
    lower = (rows_at > cols_at).astype(jnp.float32)
    identity = (rows_at == cols_at).astype(jnp.float32)
    levels = jax.random.uniform(second, (PANEL, GROUPS, PANEL), jnp.float32, 1.0, 2.0)
    values = noise * lower * (1.5 / jnp.sqrt(1.0 * PANEL)) + identity * levels
    return values.reshape(PANEL, GROUPS * PANEL).astype(jnp.bfloat16)


def plant(values, own_key, least, largest):
    longest = values.shape.index(max(values.shape))
    spots = []
    for shift in (0, 1):
        where = [jax.random.randint(jax.random.fold_in(own_key, axis), (), 0, length) for axis, length in enumerate(values.shape)]
        where[longest] = (where[longest] + shift) % values.shape[longest]
        spots.append(tuple(where))
    return values.at[spots[0]].set(least).at[spots[1]].set(largest)


def steps_of(key, dims, cuts, least, high):
    factor_of = 1.0
    for axis_at, blocks in cuts:
        draws = jax.random.uniform(jax.random.fold_in(jax.random.fold_in(key, 6), axis_at), (blocks,), jnp.float32, least / len(cuts), high / len(cuts))
        factor_of = factor_of * jnp.repeat(jnp.exp(draws), dims[axis_at] // blocks).reshape((-1,) + (1,) * (len(dims) - 1 - axis_at))
    return factor_of


def normal_values(stream_key, dims, scale, most, shards=(), held_as=jnp.bfloat16):
    array = scale * jax.random.normal(stream_key, dims, jnp.float32)
    if shards:
        array = array * steps_of(stream_key, dims, shards, -0.22, 0.18)
    return jnp.clip(array, -most, most).astype(held_as)


def setup_inputs(seed: int = 0) -> dict:
    splits = jax.random.split(jax.random.key(seed), 5)
    root_inverse = draw_root_inverse(jax.random.fold_in(splits[4], 71), 0)
    factor_panel = normal_values(splits[1], (ROOT, GROUPS * PANEL), 0.015625, 0.09375, ((0, 8), (1, 4)))
    diag_inverse = draw_diag_inverse(jax.random.fold_in(splits[4], 71), 0)
    pattern = plant((jax.random.randint(splits[3], (GROUPS, ROOT_BLOCKS), 0, 2) < 1).astype(jnp.int32), jax.random.fold_in(splits[3], 1), 0, 1)
    return dict(root_inverse=root_inverse, factor_panel=factor_panel, diag_inverse=diag_inverse, pattern=pattern)


def reference(root_inverse, factor_panel, diag_inverse, pattern):
    row_blocks = (jnp.arange(ROOT) // BLOCK).astype(jnp.int32)
    row_flags = pattern[:, row_blocks]
    keep_mask = jnp.repeat(row_flags.T, PANEL, axis=1) > 0
    masked = jnp.where(keep_mask, factor_panel, jnp.zeros_like(factor_panel))
    product = jnp.dot(root_inverse, masked, preferred_element_type=jnp.float32)
    rounded = product.astype(jnp.bfloat16)
    cross_block = jnp.where(keep_mask, -rounded, jnp.zeros_like(rounded))
    masked_groups = masked.reshape(ROOT, GROUPS, PANEL).astype(jnp.float32)
    rounded_groups = rounded.reshape(ROOT, GROUPS, PANEL).astype(jnp.float32)
    quadratic = jnp.einsum("kgi,kgj->igj", masked_groups, rounded_groups)
    factor_groups = diag_inverse.reshape(PANEL, GROUPS, PANEL).astype(jnp.float32)
    leading = jnp.einsum("kgi,kgj->igj", factor_groups, factor_groups)
    lower_mask = (jnp.arange(PANEL)[:, None, None] >= jnp.arange(PANEL)[None, None, :])
    total = leading + quadratic
    diag_block = jnp.where(lower_mask, total, jnp.zeros_like(total)).reshape(PANEL, GROUPS * PANEL)
    return cross_block, diag_block
```

```python
import functools

import jax
import jax.numpy as jnp
from jax import lax
from jax.experimental import pallas as pl
from jax.experimental.pallas import tpu as pltpu
from jax.sharding import PartitionSpec as P

BLOCK = 512
PANEL_CHUNKS = 2
ROOT_CHUNKS = 8
IN_FLIGHT = 3
MESH = pl.DeviceIdType.MESH


def ring_events(members, chunks):
    last = members // 2
    events = []
    for step in range(1, last + 1):
        for chunk in range(chunks):
            for way in (0, 1):
                if step < last or way == (0 if chunk < chunks // 2 else 1):
                    events.append((step, way, chunk))
    return events


def kernel(
    subs, blks, pattern_ref, root_ref, panel_ref, inverse_ref, cross_ref, diag_ref,
    root_all, panel_all, acc, panel_own, inverse_own, square, part, got,
    local_sem, panel_sem, inverse_sem, panel_send, panel_recv, root_send, root_recv,
    twin_send, twin_recv, own_twin_send, own_twin_recv, part_send, part_recv,
):
    rows, width = panel_ref.shape
    cols = root_ref.shape[1]
    ratio = cols // rows
    owned = diag_ref.shape[0]
    chips = subs // 2
    sub = lax.axis_index("sub")
    blk = lax.axis_index("blk")
    chip, core = sub // 2, sub % 2
    twin = chip * 2 + 1 - core

    half = blks // 2
    lane, side = blk // 2, blk % 2
    place = lane + side * (blks - 1 - 2 * lane)

    def blk_at(position):
        position = lax.rem(position + 2 * blks, blks)
        back = position // half
        return 2 * position + back * (2 * (blks - 1 - position) + 1 - 2 * position)

    def sub_at(position, which):
        return lax.rem(position + 2 * chips, chips) * 2 + which

    barrier = pltpu.get_barrier_semaphore()
    for offset in range(1, blks):
        pl.semaphore_signal(
            barrier, inc=1, device_id={"blk": lax.rem(blk + offset, blks)}, device_id_type=MESH
        )
    for offset in range(1, subs):
        pl.semaphore_signal(
            barrier, inc=1, device_id={"sub": lax.rem(sub + offset, subs)}, device_id_type=MESH
        )

    panel_fetch = pltpu.make_async_copy(panel_ref, panel_own, panel_sem)
    panel_fetch.start()
    local = pltpu.make_async_copy(root_ref, root_all.at[sub], local_sem)
    local.start()
    inverse_fetch = pltpu.make_async_copy(inverse_ref, inverse_own, inverse_sem)
    inverse_fetch.start()
    pl.semaphore_wait(barrier, blks - 1 + subs - 1)

    sign = (-1, 1)
    panel_rows = rows // PANEL_CHUNKS
    root_rows = rows // ROOT_CHUNKS
    sends = []

    def panel_copy(step, way, chunk, origin):
        region = panel_all.at[origin, pl.ds(chunk * panel_rows, panel_rows)]
        return pltpu.make_async_remote_copy(
            src_ref=region, dst_ref=region,
            send_sem=panel_send.at[way, step - 1, chunk],
            recv_sem=panel_recv.at[way, step - 1, chunk],
            device_id={"blk": blk_at(place - sign[way])}, device_id_type=MESH,
        )

    def root_copy(step, way, chunk, origin):
        here = pl.ds(chunk * root_rows, root_rows)
        region = root_all.at[origin, here]
        return pltpu.make_async_remote_copy(
            src_ref=root_ref.at[here] if step == 1 else region, dst_ref=region,
            send_sem=root_send.at[way, step - 1, chunk],
            recv_sem=root_recv.at[way, step - 1, chunk],
            device_id={"sub": sub_at(chip - sign[way], core)}, device_id_type=MESH,
        )

    def twin_copy(step, way, chunk, origin):
        region = root_all.at[origin, pl.ds(chunk * root_rows, root_rows)]
        return pltpu.make_async_remote_copy(
            src_ref=region, dst_ref=region,
            send_sem=twin_send.at[way, step - 1, chunk],
            recv_sem=twin_recv.at[way, step - 1, chunk],
            device_id={"sub": twin}, device_id_type=MESH,
        )

    panel_events = ring_events(blks, PANEL_CHUNKS)
    root_events = ring_events(chips, ROOT_CHUNKS)

    def send_panel(event):
        step, way, chunk = event
        if event in panel_events:
            copy = panel_copy(step, way, chunk, blk_at(place + sign[way] * (step - 1)))
            copy.start()
            sends.append(copy)

    def send_root(event):
        step, way, chunk = event
        if event in root_events:
            copy = root_copy(step, way, chunk, sub_at(chip + sign[way] * (step - 1), core))
            copy.start()
            sends.append(copy)

    first_sends = [event for event in root_events if event[0] == 1]
    for event in first_sends[:IN_FLIGHT]:
        send_root(event)
    piece_rows = min(rows, BLOCK)
    keeps = []
    panel_fetch.wait()
    for at in range(rows // piece_rows):
        keep = pattern_ref[0, (blk * rows + at * piece_rows) // BLOCK] > 0
        keeps.append(keep)
        here = pl.ds(at * piece_rows, piece_rows)
        values = panel_own[here, :]
        panel_all[blk, here, :] = jnp.where(keep, values, jnp.zeros_like(values))
    for event in panel_events:
        if event[0] == 1:
            send_panel(event)
    own_twin = pltpu.make_async_remote_copy(
        src_ref=root_ref, dst_ref=root_all.at[sub], send_sem=own_twin_send, recv_sem=own_twin_recv,
        device_id={"sub": twin}, device_id_type=MESH,
    )
    own_twin.start()
    sends.append(own_twin)

    tile = min(rows, 256)
    acc[...] = jnp.zeros_like(acc)

    def near_dot(origin):
        source = origin // ratio

        @pl.when(source // 2 == chip)
        def _():
            columns = pl.ds(pl.multiple_of((origin % ratio) * rows, rows), rows)

            @pl.loop(0, rows // tile)
            def _(at):
                here = pl.ds(pl.multiple_of(at * tile, tile), tile)
                acc[here, :] += jnp.dot(
                    root_all[source, here, columns], panel_all[origin],
                    preferred_element_type=jnp.float32,
                )

    def arrive_root(event):
        step, way, chunk = event
        origin = sub_at(chip + sign[way] * step, core)
        wait_root(event, origin)
        send_root((step + 1, way, chunk))
        if step == 1 and first_sends.index(event) + IN_FLIGHT < len(first_sends):
            send_root(first_sends[first_sends.index(event) + IN_FLIGHT])
        forward = twin_copy(step, way, chunk, origin)
        forward.start()
        sends.append(forward)

    def wait_root(event, origin):
        step, way, chunk = event
        region = root_all.at[origin, pl.ds(chunk * root_rows, root_rows)]
        pltpu.make_async_remote_copy(
            src_ref=region, dst_ref=region,
            send_sem=root_send.at[way, step - 1, chunk],
            recv_sem=root_recv.at[way, step - 1, chunk],
            device_id={"sub": sub_at(chip - sign[way], core)}, device_id_type=MESH,
        ).wait_recv()

    def arrive_panel(event):
        step, way, chunk = event
        panel_copy(step, way, chunk, blk_at(place + sign[way] * step)).wait_recv()
        send_panel((step + 1, way, chunk))

    merged = []
    for at, event in enumerate(panel_events):
        merged.append((0.87 * (at + 1) / len(panel_events), 0, event))
    for at, event in enumerate(root_events[:-2]):
        merged.append(((at + 1) / len(root_events), 1, event))
    merged.sort()

    contract_rows = (((0,), (0,)), ((), ()))
    inverse_fetch.wait()
    square[...] = lax.dot_general(
        inverse_own[...], inverse_own[...], contract_rows, preferred_element_type=jnp.float32
    )
    local.wait()
    pltpu.make_async_remote_copy(
        src_ref=root_ref, dst_ref=root_all.at[twin], send_sem=own_twin_send, recv_sem=own_twin_recv,
        device_id={"sub": twin}, device_id_type=MESH,
    ).wait_recv()
    near_dot(blk)
    for _, kind, event in merged:
        if kind == 1:
            arrive_root(event)
            continue
        arrive_panel(event)
        step, way, chunk = event
        if chunk == PANEL_CHUNKS - 1:
            if step == half:
                near_dot(blk_at(place + half))
            else:
                near_dot(blk_at(place + sign[way] * step))

    last = chips // 2

    def far_dot(events):
        step, way, chunk = events[0]
        origin = sub_at(chip + sign[way] * step, core)
        other = sub_at(chip + sign[way] * step, 1 - core)
        for event in events:
            twin_copy(*event, other).wait_recv()
        here = pl.ds(chunk * root_rows, len(events) * root_rows)
        total = acc[here, :]
        for source in (origin, other):
            for at in range(ratio):
                total += jnp.dot(
                    root_all[source, here, at * rows:(at + 1) * rows], panel_all[source * ratio + at],
                    preferred_element_type=jnp.float32,
                )
        if step < last:
            acc[here, :] = total
            return
        rounded = total.astype(jnp.bfloat16)
        keep = keeps[chunk * root_rows // piece_rows]
        cross_ref[here, :] = jnp.where(keep, -rounded, jnp.zeros_like(rounded))
        square[...] += lax.dot_general(
            panel_all[blk, here, :], rounded, contract_rows, preferred_element_type=jnp.float32
        )

    for step in range(1, last + 1):
        for way in (0, 1):
            chunks = [event for event in root_events if event[:2] == (step, way)]
            for at in range(0, len(chunks), 2):
                if (step, way, chunks[at][2]) == (last, 1, ROOT_CHUNKS - 2):
                    for event in root_events[-2:]:
                        arrive_root(event)
                        far_dot([event])
                else:
                    far_dot(chunks[at:at + 2])

    part[...] = square[...].astype(jnp.bfloat16).reshape(blks, owned, width)
    for offset in range(1, blks):
        target = lax.rem(blk + offset, blks)
        copy = pltpu.make_async_remote_copy(
            src_ref=part.at[target], dst_ref=got.at[offset - 1],
            send_sem=part_send.at[offset - 1], recv_sem=part_recv.at[offset - 1],
            device_id={"blk": target}, device_id_type=MESH,
        )
        copy.start()
        sends.append(copy)
    total = part[blk].astype(jnp.float32)
    for offset in range(1, blks):
        sends[offset - blks].wait_recv()
        total += got[offset - 1].astype(jnp.float32)
    rows_at = blk * owned + lax.broadcasted_iota(jnp.int32, (owned, width), 0)
    cols_at = lax.broadcasted_iota(jnp.int32, (owned, width), 1)
    diag_ref[...] = jnp.where(cols_at <= rows_at, total, jnp.zeros_like(total))
    for copy in sends:
        copy.wait_send()


def local(subs, blks, root_inverse, factor_panel, diag_inverse, pattern):
    rows, width = factor_panel.shape
    cols = root_inverse.shape[1]
    owned = diag_inverse.shape[0]
    dma = pltpu.SemaphoreType.DMA
    panel_sems = dma((2, blks // 2, PANEL_CHUNKS))
    root_sems = dma((2, subs // 4, ROOT_CHUNKS))
    hbm = pl.BlockSpec(memory_space=pl.ANY)
    vmem = pl.BlockSpec(memory_space=pltpu.VMEM)
    return pl.pallas_call(
        functools.partial(kernel, subs, blks),
        out_shape=(
            jax.ShapeDtypeStruct((rows, width), jnp.bfloat16),
            jax.ShapeDtypeStruct((owned, width), jnp.float32),
        ),
        in_specs=[
            pl.BlockSpec(memory_space=pltpu.SMEM), hbm, hbm, hbm,
        ],
        out_specs=(vmem, vmem),
        scratch_shapes=[
            pltpu.VMEM((subs, rows, cols), jnp.bfloat16),
            pltpu.VMEM((blks, rows, width), jnp.bfloat16),
            pltpu.VMEM((rows, width), jnp.float32),
            pltpu.VMEM((rows, width), jnp.bfloat16),
            pltpu.VMEM((owned, width), jnp.bfloat16),
            pltpu.VMEM((width, width), jnp.float32),
            pltpu.VMEM((blks, owned, width), jnp.bfloat16),
            pltpu.VMEM((blks - 1, owned, width), jnp.bfloat16),
            dma(()), dma(()), dma(()), panel_sems, panel_sems, root_sems, root_sems, root_sems, root_sems, dma(()), dma(()),
            dma((blks - 1,)), dma((blks - 1,)),
        ],
        compiler_params=pltpu.CompilerParams(
            collective_id=0, has_side_effects=True, vmem_limit_bytes=60 * 1024 * 1024
        ),
    )(pattern, root_inverse, factor_panel, diag_inverse)


SUB = 2
TILE = 256
(TWIN, UPDOWN, ACROSS, LIFT, SIDE_A, DROP, LIFT_A, LIFT_B, TOP, TOP_SIDE, LIFT_SIDE, HOP, VIA, VIA_HOP, HOP_SIDE_A,
 HOP_SIDE_B, HOP_UP_A, HOP_UP_B, SUM_SIDE, SUM_A, SUM_B, SUM_HOME, PAIR, BACK_A, BACK_B) = range(25)
ROWS = (((0,), (0,)), ((), ()))


def plane_kernel(
    pattern_ref, root_ref, panel_ref, inverse_ref, cross_ref, diag_ref,
    root, panel, inverse, own, gathered, mine, relay, acc, staged, twin_in, outer, outer_in, col, col_in,
    square, part, got, root_sem, panel_sem, inverse_sem, send_sem, recv_sem, part_send, part_recv,
):
    rows, width = panel_ref.shape
    half = width // 2
    owned = diag_ref.shape[0]
    blks = width // owned
    tile = min(rows, TILE)
    piece = rows // SUB
    sub, blk = lax.axis_index("sub"), lax.axis_index("blk")
    x, core_at, z_at, y = sub // 2, sub % 2, blk // 2, blk % 2
    level = z_at + x * (3 - 2 * z_at)
    core = core_at + x * (1 - 2 * core_at)

    def device(level_to, y_to, core_to, plane):
        return {
            "sub": plane * 2 + core_to + plane * (1 - 2 * core_to),
            "blk": (level_to + plane * (3 - 2 * level_to)) * 2 + y_to,
        }

    def here(level_to, y_to, core_to):
        return lambda: device(level_to, y_to, core_to, x)

    def there(level_to, y_to, core_to):
        return lambda: device(level_to, y_to, core_to, 1 - x)

    def twin():
        return {"sub": x * 2 + 1 - core_at}

    far = 1 - y

    barrier = pltpu.get_barrier_semaphore()
    for offset in range(1, 2 * blks):
        other = lax.rem(core_at * blks + blk + offset, 2 * blks)
        pl.semaphore_signal(
            barrier, inc=1, device_id={"sub": x * 2 + other // blks, "blk": other % blks}, device_id_type=MESH
        )
    for offset in range(2):
        pl.semaphore_signal(barrier, inc=1, device_id={"sub": (1 - x) * 2 + offset}, device_id_type=MESH)

    panel_fetch = pltpu.make_async_copy(panel_ref, panel, panel_sem)
    panel_fetch.start()
    root_fetch = pltpu.make_async_copy(root_ref, root, root_sem)
    root_fetch.start()
    inverse_fetch = pltpu.make_async_copy(inverse_ref, inverse, inverse_sem)
    inverse_fetch.start()

    sends = {(level_of, core_of): [] for level_of in range(4) for core_of in range(2)}

    def at(level_of, core_of, body):
        pl.when((level == level_of) & (core == core_of))(body)

    def copy(kind, j, s, source, target, to):
        return pltpu.make_async_remote_copy(
            src_ref=source, dst_ref=target, send_sem=send_sem.at[kind, j, s], recv_sem=recv_sem.at[kind, j, s],
            device_id=to(), device_id_type=MESH,
        )

    def send(key, kind, j, s, source, target, to):
        def make():
            return copy(kind, j, s, source(), target(), to)

        make().start()
        sends[key].append(make)

    def wait(kind, j, s, region):
        copy(kind, j, s, region, region, twin).wait_recv()

    def cut(s):
        return pl.ds(s * piece, piece)

    def block(q, j, y_of, s):
        return gathered.at[q, j, y_of, cut(s)]

    def pass_on(key, kind, j, s, q, y_of, to):
        send(key, kind, j, s, lambda: block(q, j, y_of, s), lambda: block(q, j, y_of, s), to)

    def own_sends(j):
        g, h = j // 2, j % 2

        def give(key, kind, s, target, to):
            send(key, kind, j, s, lambda: own.at[h, cut(s)], target, to)

        def low(level_of):
            key = (level_of, g)

            def body():
                for s in range(SUB):
                    place = functools.partial(block, 0, j, y, s)
                    if g != level_of:
                        give(key, TWIN, s, place, twin)
                    if level_of == 1:
                        give(key, LIFT, s, place, here(2, y, 1))
                    give(key, UPDOWN, s, place, here(1 - level_of, y, level_of))
                    give(key, ACROSS, s, place, here(level_of, far, level_of))
            at(level_of, g, body)

        def high(level_of):
            key = (level_of, g)

            def body():
                for s in range(SUB):
                    give(key, TWIN, s, lambda: mine.at[j, cut(s)], twin)
                for s in range(SUB):
                    if level_of == 2:
                        give(key, VIA, s, lambda: relay.at[h, cut(s)], here(3, y, g))
                    give(key, HOP, s, functools.partial(block, 1, j, y, s), there(3 - level_of, y, 3 - level_of))
            at(level_of, g, body)

        for level_of in (0, 1):
            low(level_of)
        for level_of in (2, 3):
            high(level_of)

    def forwards(j):
        g, h = j // 2, j % 2

        def low_00():
            for s in range(SUB):
                wait(HOP, j, s, block(1, j, y, s))
                pass_on((0, 0), HOP_SIDE_A, j, s, 1, y, here(0, far, 0))
                pass_on((0, 0), HOP_UP_A, j, s, 1, y, here(1, y, 0))
            for s in range(SUB):
                wait(HOP_SIDE_A, j, s, block(1, j, far, s))
                pass_on((0, 0), HOP_UP_B, j, s, 1, far, here(1, y, 0))

        def low_01():
            for s in range(SUB):
                wait(VIA_HOP, j, s, block(1, j, y, s))
                pass_on((0, 1), HOP_SIDE_A, j, s, 1, y, here(0, far, 1))

        def low_10():
            for s in range(SUB):
                wait(UPDOWN, j, s, block(0, j, y, s))
                pass_on((1, 0), LIFT_A, j, s, 0, y, here(2, y, 0))
                pass_on((1, 0), SIDE_A, j, s, 0, y, here(1, far, 0))

        def low_11():
            for s in range(SUB):
                wait(HOP, j, s, block(1, j, y, s))
                pass_on((1, 1), HOP_SIDE_B, j, s, 1, y, here(1, far, 1))
            for s in range(SUB):
                wait(ACROSS, j, s, block(0, j, far, s))
                pass_on((1, 1), LIFT_B, j, s, 0, far, here(2, y, 1))
                pass_on((1, 1), DROP, j, s, 0, far, here(0, y, 1))

        def high_20():
            for s in range(SUB):
                wait(LIFT_A, j, s, block(0, j, y, s))
                pass_on((2, 0), TOP, j, s, 0, y, here(3, y, 0))
                pass_on((2, 0), LIFT_SIDE, j, s, 0, y, here(2, far, 0))

        def high_21():
            for s in range(SUB):
                wait(LIFT, j, s, block(0, j, y, s))
                pass_on((2, 1), TOP, j, s, 0, y, here(3, y, 1))

        def high_3(core_of):
            def body():
                if core_of == g:
                    for s in range(SUB):
                        wait(VIA, j, s, relay.at[h, cut(s)])
                        send(
                            (3, g), VIA_HOP, j, s, lambda: relay.at[h, cut(s)], lambda: block(1, j, y, s),
                            there(0, y, 1),
                        )
                for s in range(SUB):
                    wait(TOP, j, s, block(0, j, y, s))
                    pass_on((3, core_of), TOP_SIDE, j, s, 0, y, here(3, far, core_of))
            return body

        at(0, 0, low_00)
        at(0, 1, low_01)
        at(1, 0, low_10)
        at(1, 1, low_11)
        at(2, 0, high_20)
        at(2, 1, high_21)
        at(3, 0, high_3(0))
        at(3, 1, high_3(1))

    def arrive(level_of, core_of, j, what):
        def body():
            for s in range(SUB):
                for kind, q, y_of in what:
                    wait(kind, j, s, block(q, j, y_of, s))
        at(level_of, core_of, body)

    def times(q, j, at_row):
        span = pl.ds(at_row, tile)
        return jnp.dot(
            root[span, :rows], gathered[q, j, 0], preferred_element_type=jnp.float32
        ) + jnp.dot(root[span, rows:], gathered[q, j, 1], preferred_element_type=jnp.float32)

    def over_rows(body):
        @pl.loop(0, rows // tile)
        def _(step):
            body(pl.multiple_of(step * tile, tile))

    def outer_work(j):
        g, h = j // 2, j % 2
        arrive(0, 1, j, [(HOP_SIDE_A, 1, far)])
        arrive(1, 0, j, [(HOP_UP_A, 1, y), (HOP_UP_B, 1, far)])
        arrive(1, 1, j, [(HOP_SIDE_B, 1, far)])

        @pl.when(level < 2)
        def _():
            def body(at_row):
                outer[j, pl.ds(at_row, tile)] = times(1, j, at_row).astype(jnp.bfloat16)
            over_rows(body)

        for level_of in (0, 1):
            for core_of in (0, 1):
                def back(level_of=level_of, core_of=core_of):
                    for s in range(SUB):
                        send(
                            (level_of, core_of), BACK_A + core_of, j, s, lambda: outer.at[j, cut(s)],
                            lambda: outer_in.at[core_of, h, cut(s)], there(3 - level_of, y, g),
                        )
                at(level_of, core_of, back)

    def col_work(j):
        g = j // 2

        @pl.when((level >= 2) & (core != g))
        def _():
            for s in range(SUB):
                wait(TWIN, j, s, mine.at[j, cut(s)])

        @pl.when(level >= 2)
        def _():
            for y_of in range(2):
                def body(at_row):
                    columns = pl.ds(y_of * rows + at_row, tile)
                    col[j, y_of, pl.ds(at_row, tile)] = lax.dot_general(
                        root[:, columns], mine[j], ROWS, preferred_element_type=jnp.float32
                    ).astype(jnp.bfloat16)
                over_rows(body)

        def sum_send(key, kind, slot, y_of, to):
            for s in range(SUB):
                send(key, kind, j, s, lambda: col.at[j, y_of, cut(s)], lambda: col_in.at[slot, j, cut(s)], to)

        at(2, 0, lambda: sum_send((2, 0), SUM_SIDE, 0, far, here(2, far, 0)))
        at(3, 0, lambda: sum_send((3, 0), SUM_SIDE, 0, far, here(3, far, 0)))

        def top_1():
            sum_send((3, 1), SUM_B, 2, far, here(2, y, 1))
            sum_send((3, 1), SUM_A, 1, y, here(2, y, 1))
        at(3, 1, top_1)

    def add_in(j, s, y_of, slots):
        total = col[j, y_of, cut(s)].astype(jnp.float32)
        for slot in slots:
            total += col_in[slot, j, cut(s)].astype(jnp.float32)
        col[j, y_of, cut(s)] = total.astype(jnp.bfloat16)

    def sum_first(j):
        def top_0():
            for s in range(SUB):
                wait(SUM_SIDE, j, s, col_in.at[0, j, cut(s)])
                add_in(j, s, y, (0,))
                send(
                    (3, 0), SUM_A, j, s, lambda: col.at[j, y, cut(s)], lambda: col_in.at[1, j, cut(s)], here(2, y, 0)
                )

        def mid_1():
            for s in range(SUB):
                wait(SUM_B, j, s, col_in.at[2, j, cut(s)])
                add_in(j, s, far, (2,))
                send(
                    (2, 1), SUM_SIDE, j, s, lambda: col.at[j, far, cut(s)], lambda: col_in.at[0, j, cut(s)],
                    here(2, far, 1),
                )
        at(3, 0, top_0)
        at(2, 1, mid_1)

    def sum_last(j):
        g, h = j // 2, j % 2

        def mid(core_of):
            def body():
                for s in range(SUB):
                    wait(SUM_A, j, s, col_in.at[1, j, cut(s)])
                    wait(SUM_SIDE, j, s, col_in.at[0, j, cut(s)])
                    add_in(j, s, y, (0, 1))
                    send(
                        (2, core_of), SUM_HOME, j, s, lambda: col.at[j, y, cut(s)],
                        lambda: outer_in.at[0, h, cut(s)], here(core_of, y, g),
                    )
            return body
        at(2, 0, mid(0))
        at(2, 1, mid(1))

    def inner_work(j):
        g, h = j // 2, j % 2
        arrive(0, 0, j, [(ACROSS, 0, far)] + ([(TWIN, 0, y)] if g != 0 else []))
        arrive(0, 1, j, [(UPDOWN, 0, y), (DROP, 0, far)])
        arrive(1, 0, j, [(SIDE_A, 0, far)])
        if g != 1:
            arrive(1, 1, j, [(TWIN, 0, y)])
        arrive(2, 0, j, [(LIFT_SIDE, 0, far)])
        arrive(2, 1, j, [(LIFT_B, 0, far)])
        for core_of in (0, 1):
            arrive(3, core_of, j, [(TOP_SIDE, 0, far)])

        def body(at_row):
            span = pl.ds(at_row, tile)
            value = times(0, j, at_row)
            acc[h, span] = value
            staged[j, span] = value.astype(jnp.bfloat16)
        over_rows(body)

        for level_of in range(4):
            def pair(level_of=level_of):
                for s in range(SUB):
                    send(
                        (level_of, 1 - g), PAIR, j, s, lambda: staged.at[j, cut(s)],
                        lambda: twin_in.at[h, cut(s)], twin,
                    )
            at(level_of, 1 - g, pair)

    keeps = []
    keep_rows = min(rows, BLOCK)

    def finish(j):
        g, h = j // 2, j % 2

        @pl.when(core == g)
        def _():
            for s in range(SUB):
                wait(PAIR, j, s, twin_in.at[h, cut(s)])

            @pl.when(level < 2)
            def _():
                for s in range(SUB):
                    wait(SUM_HOME, j, s, outer_in.at[0, h, cut(s)])

                def body(at_row):
                    span = pl.ds(at_row, tile)
                    acc[h, span] += outer_in[0, h, span].astype(jnp.float32)
                over_rows(body)

            @pl.when(level >= 2)
            def _():
                for s in range(SUB):
                    for k in range(2):
                        wait(BACK_A + k, j, s, outer_in.at[k, h, cut(s)])

                def body(at_row):
                    span = pl.ds(at_row, tile)
                    acc[h, span] += outer_in[0, h, span].astype(jnp.float32) + outer_in[1, h, span].astype(jnp.float32)
                over_rows(body)

            for step in range(rows // tile):
                span = pl.ds(step * tile, tile)
                rounded = (acc[h, span] + twin_in[h, span].astype(jnp.float32)).astype(jnp.bfloat16)
                keep = keeps[step * tile // keep_rows]
                cross_ref[span, h * half:(h + 1) * half] = jnp.where(keep, -rounded, jnp.zeros_like(rounded))
                for a in range(h, 2):
                    square[a * half:(a + 1) * half, h * half:(h + 1) * half] += lax.dot_general(
                        own[a, span], rounded, ROWS, preferred_element_type=jnp.float32
                    )

    def part_copy(offset):
        target = lax.rem(blk + offset, blks)
        return pltpu.make_async_remote_copy(
            src_ref=part.at[target], dst_ref=got.at[offset - 1],
            send_sem=part_send.at[offset - 1], recv_sem=part_recv.at[offset - 1],
            device_id={"blk": target}, device_id_type=MESH,
        )

    def part_sends(g):
        @pl.when(core == g)
        def _():
            part[...] = square[...].astype(jnp.bfloat16).reshape(blks, owned, width)
            for offset in range(1, blks):
                part_copy(offset).start()

    panel_fetch.wait()
    for step in range(rows // keep_rows):
        keep = pattern_ref[0, (blk * rows + step * keep_rows) // BLOCK] > 0
        keeps.append(keep)
        span = pl.ds(step * keep_rows, keep_rows)
        for h in range(2):
            values = panel[span, h * half:(h + 1) * half]
            values = jnp.where(keep, values, jnp.zeros_like(values))
            own[h, span] = values

            @pl.when(level >= 2)
            def _():
                mine[2 * core + h, span] = values

            @pl.when(level == core)
            def _():
                gathered[0, 2 * core + h, y, span] = values
    pl.semaphore_wait(barrier, 2 * blks + 1)
    own_sends(0)
    inverse_fetch.wait()
    square[...] = lax.dot_general(inverse[...], inverse[...], ROWS, preferred_element_type=jnp.float32)
    root_fetch.wait()
    col_work(0)
    for j in range(4):
        if j < 3:
            own_sends(j + 1)
        sum_first(j)
        forwards(j)
        outer_work(j)
        sum_last(j)
        if j < 3:
            col_work(j + 1)
        inner_work(j)
        if j >= 1:
            finish(j - 1)
        if j == 2:
            part_sends(0)
    finish(3)
    part_sends(1)
    total = part[blk].astype(jnp.float32)
    for offset in range(1, blks):
        part_copy(offset).wait_recv()
        total += got[offset - 1].astype(jnp.float32)
    rows_at = blk * owned + lax.broadcasted_iota(jnp.int32, (owned, width), 0)
    cols_at = lax.broadcasted_iota(jnp.int32, (owned, width), 1)
    diag_ref[...] = jnp.where(cols_at <= rows_at, total, jnp.zeros_like(total))
    for offset in range(1, blks):
        part_copy(offset).wait_send()
    for (level_of, core_of), makes in sends.items():
        def drain(makes=makes):
            for make in makes:
                make().wait_send()
        at(level_of, core_of, drain)


def plane_local(blks, root_inverse, factor_panel, diag_inverse, pattern):
    rows, width = factor_panel.shape
    half = width // 2
    owned = diag_inverse.shape[0]
    dma = pltpu.SemaphoreType.DMA
    hbm = pl.BlockSpec(memory_space=pl.ANY)
    vmem = pl.BlockSpec(memory_space=pltpu.VMEM)

    def held(*lead, dtype=jnp.bfloat16):
        return pltpu.VMEM((*lead, rows, half), dtype)

    return pl.pallas_call(
        plane_kernel,
        out_shape=(
            jax.ShapeDtypeStruct((rows, width), jnp.bfloat16),
            jax.ShapeDtypeStruct((owned, width), jnp.float32),
        ),
        in_specs=[pl.BlockSpec(memory_space=pltpu.SMEM), hbm, hbm, hbm],
        out_specs=(vmem, vmem),
        scratch_shapes=[
            pltpu.VMEM(root_inverse.shape, jnp.bfloat16),
            pltpu.VMEM((rows, width), jnp.bfloat16),
            pltpu.VMEM((owned, width), jnp.bfloat16),
            held(2), held(2, 4, 2), held(4), held(2), held(2, dtype=jnp.float32), held(4), held(2),
            held(4), held(2, 2), held(4, 2), held(3, 4),
            pltpu.VMEM((width, width), jnp.float32),
            pltpu.VMEM((blks, owned, width), jnp.bfloat16),
            pltpu.VMEM((blks - 1, owned, width), jnp.bfloat16),
            dma(()), dma(()), dma(()), dma((25, 4, SUB)), dma((25, 4, SUB)), dma((blks - 1,)), dma((blks - 1,)),
        ],
        compiler_params=pltpu.CompilerParams(
            collective_id=1, has_side_effects=True, vmem_limit_bytes=60 * 1024 * 1024
        ),
    )(pattern, root_inverse, factor_panel, diag_inverse)


def fits(mesh, root_inverse, factor_panel):
    subs, blks = mesh.shape["sub"], mesh.shape["blk"]
    rows, columns = root_inverse.shape
    return (subs, blks) == (4, 8) and factor_panel.shape[1] % (4 * 256) == 0 and rows % (blks * BLOCK) == 0


def solution(mesh):
    subs, blks = mesh.shape["sub"], mesh.shape["blk"]

    def run(root_inverse, factor_panel, diag_inverse, pattern):
        body = functools.partial(local, subs, blks)
        if fits(mesh, root_inverse, factor_panel):
            body = functools.partial(plane_local, blks)
        return jax.shard_map(
            body,
            mesh=mesh,
            in_specs=(P("blk", "sub"), P("blk", "sub"), P("blk", "sub"), P("sub", None)),
            out_specs=(P("blk", "sub"), P("blk", "sub")),
            check_vma=False,
        )(root_inverse, factor_panel, diag_inverse, pattern)

    return run
```

```python
import functools

import jax
import jax.numpy as jnp
from jax import lax
from jax.experimental import pallas as pl
from jax.experimental.pallas import tpu as pltpu
from jax.sharding import PartitionSpec as P

BLOCK = 512
PANEL_CHUNKS = 2
ROOT_CHUNKS = 8
IN_FLIGHT = 3
MESH = pl.DeviceIdType.MESH


def ring_events(members, chunks):
    last = members // 2
    events = []
    for step in range(1, last + 1):
        for chunk in range(chunks):
            for way in (0, 1):
                if step < last or way == (0 if chunk < chunks // 2 else 1):
                    events.append((step, way, chunk))
    return events


def kernel(
    subs, blks, pattern_ref, root_ref, panel_ref, inverse_ref, cross_ref, diag_ref,
    root_all, panel_all, acc, panel_own, inverse_own, square, part, got,
    local_sem, panel_sem, inverse_sem, panel_send, panel_recv, root_send, root_recv,
    twin_send, twin_recv, own_twin_send, own_twin_recv, part_send, part_recv,
):
    rows, width = panel_ref.shape
    cols = root_ref.shape[1]
    ratio = cols // rows
    owned = diag_ref.shape[0]
    chips = subs // 2
    sub = lax.axis_index("sub")
    blk = lax.axis_index("blk")
    chip, core = sub // 2, sub % 2
    twin = chip * 2 + 1 - core

    half = blks // 2
    lane, side = blk // 2, blk % 2
    place = lane + side * (blks - 1 - 2 * lane)

    def blk_at(position):
        position = lax.rem(position + 2 * blks, blks)
        back = position // half
        return 2 * position + back * (2 * (blks - 1 - position) + 1 - 2 * position)

    def sub_at(position, which):
        return lax.rem(position + 2 * chips, chips) * 2 + which

    barrier = pltpu.get_barrier_semaphore()
    for offset in range(1, blks):
        pl.semaphore_signal(
            barrier, inc=1, device_id={"blk": lax.rem(blk + offset, blks)}, device_id_type=MESH
        )
    for offset in range(1, subs):
        pl.semaphore_signal(
            barrier, inc=1, device_id={"sub": lax.rem(sub + offset, subs)}, device_id_type=MESH
        )

    panel_fetch = pltpu.make_async_copy(panel_ref, panel_own, panel_sem)
    panel_fetch.start()
    local = pltpu.make_async_copy(root_ref, root_all.at[sub], local_sem)
    local.start()
    inverse_fetch = pltpu.make_async_copy(inverse_ref, inverse_own, inverse_sem)
    inverse_fetch.start()
    pl.semaphore_wait(barrier, blks - 1 + subs - 1)

    sign = (-1, 1)
    panel_rows = rows // PANEL_CHUNKS
    root_rows = rows // ROOT_CHUNKS
    sends = []

    def panel_copy(step, way, chunk, origin):
        region = panel_all.at[origin, pl.ds(chunk * panel_rows, panel_rows)]
        return pltpu.make_async_remote_copy(
            src_ref=region, dst_ref=region,
            send_sem=panel_send.at[way, step - 1, chunk],
            recv_sem=panel_recv.at[way, step - 1, chunk],
            device_id={"blk": blk_at(place - sign[way])}, device_id_type=MESH,
        )

    def root_copy(step, way, chunk, origin):
        here = pl.ds(chunk * root_rows, root_rows)
        region = root_all.at[origin, here]
        return pltpu.make_async_remote_copy(
            src_ref=root_ref.at[here] if step == 1 else region, dst_ref=region,
            send_sem=root_send.at[way, step - 1, chunk],
            recv_sem=root_recv.at[way, step - 1, chunk],
            device_id={"sub": sub_at(chip - sign[way], core)}, device_id_type=MESH,
        )

    def twin_copy(step, way, chunk, origin):
        region = root_all.at[origin, pl.ds(chunk * root_rows, root_rows)]
        return pltpu.make_async_remote_copy(
            src_ref=region, dst_ref=region,
            send_sem=twin_send.at[way, step - 1, chunk],
            recv_sem=twin_recv.at[way, step - 1, chunk],
            device_id={"sub": twin}, device_id_type=MESH,
        )

    panel_events = ring_events(blks, PANEL_CHUNKS)
    root_events = ring_events(chips, ROOT_CHUNKS)

    def send_panel(event):
        step, way, chunk = event
        if event in panel_events:
            copy = panel_copy(step, way, chunk, blk_at(place + sign[way] * (step - 1)))
            copy.start()
            sends.append(copy)

    def send_root(event):
        step, way, chunk = event
        if event in root_events:
            copy = root_copy(step, way, chunk, sub_at(chip + sign[way] * (step - 1), core))
            copy.start()
            sends.append(copy)

    first_sends = [event for event in root_events if event[0] == 1]
    for event in first_sends[:IN_FLIGHT]:
        send_root(event)
    piece_rows = min(rows, BLOCK)
    keeps = []
    panel_fetch.wait()
    for at in range(rows // piece_rows):
        keep = pattern_ref[0, (blk * rows + at * piece_rows) // BLOCK] > 0
        keeps.append(keep)
        here = pl.ds(at * piece_rows, piece_rows)
        values = panel_own[here, :]
        panel_all[blk, here, :] = jnp.where(keep, values, jnp.zeros_like(values))
    for event in panel_events:
        if event[0] == 1:
            send_panel(event)
    own_twin = pltpu.make_async_remote_copy(
        src_ref=root_ref, dst_ref=root_all.at[sub], send_sem=own_twin_send, recv_sem=own_twin_recv,
        device_id={"sub": twin}, device_id_type=MESH,
    )
    own_twin.start()
    sends.append(own_twin)

    tile = min(rows, 256)
    acc[...] = jnp.zeros_like(acc)

    def near_dot(origin):
        source = origin // ratio

        @pl.when(source // 2 == chip)
        def _():
            columns = pl.ds(pl.multiple_of((origin % ratio) * rows, rows), rows)

            @pl.loop(0, rows // tile)
            def _(at):
                here = pl.ds(pl.multiple_of(at * tile, tile), tile)
                acc[here, :] += jnp.dot(
                    root_all[source, here, columns], panel_all[origin],
                    preferred_element_type=jnp.float32,
                )

    def arrive_root(event):
        step, way, chunk = event
        origin = sub_at(chip + sign[way] * step, core)
        wait_root(event, origin)
        send_root((step + 1, way, chunk))
        if step == 1 and first_sends.index(event) + IN_FLIGHT < len(first_sends):
            send_root(first_sends[first_sends.index(event) + IN_FLIGHT])
        forward = twin_copy(step, way, chunk, origin)
        forward.start()
        sends.append(forward)

    def wait_root(event, origin):
        step, way, chunk = event
        region = root_all.at[origin, pl.ds(chunk * root_rows, root_rows)]
        pltpu.make_async_remote_copy(
            src_ref=region, dst_ref=region,
            send_sem=root_send.at[way, step - 1, chunk],
            recv_sem=root_recv.at[way, step - 1, chunk],
            device_id={"sub": sub_at(chip - sign[way], core)}, device_id_type=MESH,
        ).wait_recv()

    def arrive_panel(event):
        step, way, chunk = event
        panel_copy(step, way, chunk, blk_at(place + sign[way] * step)).wait_recv()
        send_panel((step + 1, way, chunk))

    merged = []
    for at, event in enumerate(panel_events):
        merged.append((0.87 * (at + 1) / len(panel_events), 0, event))
    for at, event in enumerate(root_events[:-2]):
        merged.append(((at + 1) / len(root_events), 1, event))
    merged.sort()

    contract_rows = (((0,), (0,)), ((), ()))
    inverse_fetch.wait()
    square[...] = lax.dot_general(
        inverse_own[...], inverse_own[...], contract_rows, preferred_element_type=jnp.float32
    )
    local.wait()
    pltpu.make_async_remote_copy(
        src_ref=root_ref, dst_ref=root_all.at[twin], send_sem=own_twin_send, recv_sem=own_twin_recv,
        device_id={"sub": twin}, device_id_type=MESH,
    ).wait_recv()
    near_dot(blk)
    for _, kind, event in merged:
        if kind == 1:
            arrive_root(event)
            continue
        arrive_panel(event)
        step, way, chunk = event
        if chunk == PANEL_CHUNKS - 1:
            if step == half:
                near_dot(blk_at(place + half))
            else:
                near_dot(blk_at(place + sign[way] * step))

    last = chips // 2

    def far_dot(events):
        step, way, chunk = events[0]
        origin = sub_at(chip + sign[way] * step, core)
        other = sub_at(chip + sign[way] * step, 1 - core)
        for event in events:
            twin_copy(*event, other).wait_recv()
        here = pl.ds(chunk * root_rows, len(events) * root_rows)
        total = acc[here, :]
        for source in (origin, other):
            for at in range(ratio):
                total += jnp.dot(
                    root_all[source, here, at * rows:(at + 1) * rows], panel_all[source * ratio + at],
                    preferred_element_type=jnp.float32,
                )
        if step < last:
            acc[here, :] = total
            return
        rounded = total.astype(jnp.bfloat16)
        keep = keeps[chunk * root_rows // piece_rows]
        cross_ref[here, :] = jnp.where(keep, -rounded, jnp.zeros_like(rounded))
        square[...] += lax.dot_general(
            panel_all[blk, here, :], rounded, contract_rows, preferred_element_type=jnp.float32
        )

    for step in range(1, last + 1):
        for way in (0, 1):
            chunks = [event for event in root_events if event[:2] == (step, way)]
            for at in range(0, len(chunks), 2):
                if (step, way, chunks[at][2]) == (last, 1, ROOT_CHUNKS - 2):
                    for event in root_events[-2:]:
                        arrive_root(event)
                        far_dot([event])
                else:
                    far_dot(chunks[at:at + 2])

    part[...] = square[...].astype(jnp.bfloat16).reshape(blks, owned, width)
    for offset in range(1, blks):
        target = lax.rem(blk + offset, blks)
        copy = pltpu.make_async_remote_copy(
            src_ref=part.at[target], dst_ref=got.at[offset - 1],
            send_sem=part_send.at[offset - 1], recv_sem=part_recv.at[offset - 1],
            device_id={"blk": target}, device_id_type=MESH,
        )
        copy.start()
        sends.append(copy)
    total = part[blk].astype(jnp.float32)
    for offset in range(1, blks):
        sends[offset - blks].wait_recv()
        total += got[offset - 1].astype(jnp.float32)
    rows_at = blk * owned + lax.broadcasted_iota(jnp.int32, (owned, width), 0)
    cols_at = lax.broadcasted_iota(jnp.int32, (owned, width), 1)
    diag_ref[...] = jnp.where(cols_at <= rows_at, total, jnp.zeros_like(total))
    for copy in sends:
        copy.wait_send()


def local(subs, blks, root_inverse, factor_panel, diag_inverse, pattern):
    rows, width = factor_panel.shape
    cols = root_inverse.shape[1]
    owned = diag_inverse.shape[0]
    dma = pltpu.SemaphoreType.DMA
    panel_sems = dma((2, blks // 2, PANEL_CHUNKS))
    root_sems = dma((2, subs // 4, ROOT_CHUNKS))
    hbm = pl.BlockSpec(memory_space=pl.ANY)
    vmem = pl.BlockSpec(memory_space=pltpu.VMEM)
    return pl.pallas_call(
        functools.partial(kernel, subs, blks),
        out_shape=(
            jax.ShapeDtypeStruct((rows, width), jnp.bfloat16),
            jax.ShapeDtypeStruct((owned, width), jnp.float32),
        ),
        in_specs=[
            pl.BlockSpec(memory_space=pltpu.SMEM), hbm, hbm, hbm,
        ],
        out_specs=(vmem, vmem),
        scratch_shapes=[
            pltpu.VMEM((subs, rows, cols), jnp.bfloat16),
            pltpu.VMEM((blks, rows, width), jnp.bfloat16),
            pltpu.VMEM((rows, width), jnp.float32),
            pltpu.VMEM((rows, width), jnp.bfloat16),
            pltpu.VMEM((owned, width), jnp.bfloat16),
            pltpu.VMEM((width, width), jnp.float32),
            pltpu.VMEM((blks, owned, width), jnp.bfloat16),
            pltpu.VMEM((blks - 1, owned, width), jnp.bfloat16),
            dma(()), dma(()), dma(()), panel_sems, panel_sems, root_sems, root_sems, root_sems, root_sems, dma(()), dma(()),
            dma((blks - 1,)), dma((blks - 1,)),
        ],
        compiler_params=pltpu.CompilerParams(
            collective_id=0, has_side_effects=True, vmem_limit_bytes=60 * 1024 * 1024
        ),
    )(pattern, root_inverse, factor_panel, diag_inverse)


SUB = 2
TILE = 256
(
    TWIN, LIFT, UPDOWN, ACROSS, VIA, HOP, HOP_SIDE_A, HOP_UP_A, HOP_UP_B, LIFT_A, SIDE_A, HOP_SIDE_B, LIFT_B, DROP, TOP,
    LIFT_SIDE, VIA_HOP, TOP_SIDE, BACK_A, BACK_B, SUM_SIDE, SUM_B, SUM_A, SUM_HOME, PAIR,
) = range(25)
COL, OUTER, INNER, FINISH = range(4)
STEPS = (
    (COL, 0), (COL, 1), (COL, 2), (COL, 3), (OUTER, 0), (INNER, 0), (OUTER, 1), (INNER, 1), (FINISH, 0),
    (OUTER, 2), (INNER, 2), (FINISH, 1), (OUTER, 3), (INNER, 3), (FINISH, 2), (FINISH, 3),
)
PROGRAMS = (
    (
        300, 301, 200, 201, 20200, 210, 20300, 310, 20201, 211, 10500, 20301, 600, 20210, 700, 20310, 311,
        10501, 20600, 601, 20211, 701, 10510, 20311, 610, 20700, 710, 10511, 20601, 611, 20701, 711, 10600,
        20710, 800, 10601, 20711, 801, 30100, 1800, 1801, 10300, 10301, 30200, 10610, 10611, 30110, 21800,
        1810, 21801, 1811, 10310, 10311, 30210, 10520, 20610, 620, 20800, 810, 10521, 20611, 621, 20801, 811,
        20810, 720, 20811, 721, 10530, 20620, 630, 10620, 20720, 820, 10621, 20721, 821, 12400, 12401, 12300,
        12301, 30300, 10531, 20621, 631, 30120, 21810, 1820, 21811, 1821, 10320, 10321, 10020, 10021, 30220,
        2420, 2421, 12410, 12411, 12310, 12311, 30310, 20820, 730, 20821, 731, 10630, 10631, 30130, 21820,
        1830, 21821, 1831, 20730, 830, 20731, 831, 10330, 10331, 10030, 10031, 30230, 2430, 2431,
    ),
    (
        30, 31, 20, 21, 11600, 600, 11601, 601, 220, 221, 11610, 20600, 610, 11611, 20601, 611, 20610, 320,
        10600, 10601, 30100, 1900, 1901, 10200, 10201, 11300, 11301, 30200, 2400, 2401, 10610, 10611, 30110,
        21900, 1910, 21901, 1911, 10210, 10211, 11310, 11311, 30210, 2410, 2411, 20611, 330, 20320, 321, 20220,
        230, 11620, 20330, 620, 20221, 231, 20321, 331, 11621, 20620, 621, 11630, 20331, 630, 11631, 20621,
        631, 10620, 10621, 30120, 21910, 1920, 21911, 1921, 10220, 10221, 11320, 11321, 30220, 10630, 10631,
        30130, 21920, 1930, 21921, 1931, 10230, 10231, 11330, 11331, 30230, 12420, 12421, 12320, 12321, 30320,
        12430, 12431, 12330, 12331, 30330,
    ),
    (
        300, 100, 301, 101, 0, 1, 210, 211, 20300, 310, 20301, 311, 10, 11, 20210, 200, 20211, 201, 20100, 110,
        10200, 20101, 900, 20110, 111, 10201, 20900, 901, 20310, 1000, 20311, 1001, 10210, 20111, 910, 10211,
        20901, 911, 21000, 1010, 21001, 1011, 10700, 10701, 10800, 10801, 30100, 1800, 1801, 11000, 11001,
        30200, 10710, 10711, 10810, 10811, 30110, 11010, 11011, 30210, 12400, 12401, 12300, 12301, 30300,
        10220, 20910, 920, 21010, 1020, 10221, 20911, 921, 21011, 1021, 10230, 20920, 930, 21800, 1810, 10231,
        20921, 931, 21801, 1811, 10720, 10721, 10820, 10821, 30120, 21810, 1820, 21811, 1821, 11020, 11021,
        30220, 12410, 12411, 12310, 12311, 30310, 21020, 1030, 2420, 2421, 21021, 1031, 10730, 10731, 10830,
        10831, 30130, 21820, 1830, 21821, 1831, 11030, 11031, 30230, 2430, 2431,
    ),
    (
        10500, 1100, 10501, 1101, 10300, 1300, 10301, 1301, 10310, 21300, 1310, 10311, 21301, 1311, 1200,
        21310, 220, 11100, 11101, 30100, 1900, 1901, 1201, 21311, 221, 21200, 120, 10510, 21100, 1110, 21201,
        121, 10511, 21101, 1111, 10520, 21110, 1120, 20220, 230, 20120, 1210, 21111, 320, 10000, 10001, 30200,
        2400, 2401, 20121, 1211, 10521, 21120, 1121, 20221, 231, 11110, 11111, 30110, 10010, 10011, 30210,
        2410, 2411, 21210, 130, 20320, 321, 21211, 131, 21900, 1910, 10530, 21121, 1130, 21901, 1911, 11120,
        11121, 30120, 21910, 1920, 21911, 1921, 10320, 20230, 1320, 20321, 330, 10531, 21130, 1131, 20130,
        1220, 10321, 20231, 1321, 20131, 1221, 20330, 331, 10330, 21320, 1330, 21220, 1230, 10331, 21221, 1231,
        21321, 1331, 30220, 11130, 11131, 30130, 21920, 1930, 21921, 1931, 30230, 12420, 12421, 12320, 12321,
        30320, 12430, 12431, 12330, 12331, 30330,
    ),
    (
        10, 11, 400, 0, 401, 1, 500, 501, 30000, 2000, 2001, 20500, 510, 30010, 22000, 2010, 22001, 2011,
        20400, 410, 20501, 511, 10020, 10021, 30020, 10030, 10031, 30030, 20401, 411, 10900, 22010, 1500,
        22011, 2020, 10901, 21500, 1501, 22020, 2021, 12200, 12000, 2300, 20410, 1400, 12201, 12001, 2301,
        20411, 1401, 11500, 11501, 30200, 10910, 21400, 1410, 21501, 1510, 22021, 2030, 10911, 21401, 1411,
        21510, 1511, 22030, 2031, 12210, 12010, 22300, 2310, 12211, 12011, 22301, 2311, 12220, 12020, 22310,
        2320, 10920, 21511, 1520, 21410, 1420, 10921, 22031, 1521, 11510, 11511, 30210, 12400, 12401, 11800,
        11801, 11900, 11901, 30300, 21411, 1421, 12221, 12021, 22311, 2321, 10930, 21420, 1430, 12230, 12030,
        22320, 2330, 21520, 1530, 10931, 21421, 1431, 21521, 1531, 12231, 12031, 22321, 2331, 11520, 11521,
        30220, 2420, 2421, 12410, 12411, 11810, 11811, 11910, 11911, 30310, 11530, 11531, 30230, 2430, 2431,
    ),
    (
        20, 21, 30, 31, 10000, 10001, 30000, 10100, 1400, 10010, 10011, 30010, 30020, 10101, 1401, 520, 10110,
        21400, 1410, 521, 12100, 2000, 10111, 21401, 1411, 30030, 12101, 2001, 20520, 530, 20521, 531, 12200,
        12000, 2300, 21410, 420, 12201, 12001, 2301, 21411, 421, 12110, 22000, 2010, 12111, 22001, 2011, 20420,
        430, 10120, 20421, 1420, 20430, 431, 10121, 21420, 1421, 12210, 12010, 22300, 2310, 10130, 20431, 1430,
        12211, 12011, 22301, 2311, 12120, 22010, 2020, 11200, 11201, 30200, 2400, 2401, 11210, 11211, 30210,
        2410, 2411, 12220, 12020, 22310, 2320, 10131, 21421, 1431, 12121, 22011, 2021, 12130, 22020, 2030,
        12221, 12021, 22311, 2321, 12131, 22021, 2031, 11220, 11221, 30220, 12230, 12030, 22320, 2330, 11230,
        11231, 30230, 12231, 12031, 22321, 2331, 12420, 12421, 11820, 11821, 11920, 11921, 30320, 12430, 12431,
        11830, 11831, 11930, 11931, 30330,
    ),
    (
        500, 501, 10, 11, 0, 1, 30000, 2000, 2001, 30010, 10020, 10021, 30020, 22000, 2020, 22001, 2021, 20500,
        510, 20501, 511, 22020, 2010, 10400, 20510, 1600, 12000, 2200, 10030, 10031, 30030, 22021, 2011, 10401,
        20511, 1601, 22010, 2030, 12001, 2201, 10410, 21600, 1610, 12010, 22200, 2210, 10411, 21601, 1611,
        12011, 22201, 2211, 22011, 2031, 11400, 22030, 1700, 11401, 22031, 1701, 11700, 11701, 30200, 11410,
        21700, 1710, 11411, 21701, 1711, 12020, 22210, 2220, 12021, 22211, 2221, 12030, 22220, 2230, 11420,
        21710, 1720, 11710, 11711, 30210, 12400, 12401, 11800, 11801, 11900, 11901, 30300, 11421, 21711, 1721,
        12031, 22221, 2231, 11430, 21720, 1730, 11431, 21721, 1731, 11720, 11721, 30220, 2420, 2421, 12410,
        12411, 11810, 11811, 11910, 11911, 30310, 11730, 11731, 30230, 2430, 2431,
    ),
    (
        30, 31, 20, 21, 10000, 10001, 30000, 2100, 10010, 10011, 30010, 2101, 22100, 2200, 30020, 22101, 2201,
        22200, 2110, 22201, 2111, 30030, 22110, 2210, 520, 11410, 1710, 521, 22111, 2211, 22210, 2220, 11411,
        1711, 20520, 530, 11400, 21710, 1700, 22211, 2120, 20521, 531, 11401, 21711, 1701, 22220, 2121, 22120,
        2221, 10420, 20530, 1620, 10421, 20531, 1621, 11420, 21700, 1720, 11421, 21701, 1721, 22121, 2130,
        11700, 11701, 30200, 2400, 2401, 11710, 11711, 30210, 2410, 2411, 10430, 21620, 1630, 22221, 2131,
        10431, 21621, 1631, 11430, 21720, 1730, 11431, 21721, 1731, 11720, 11721, 30220, 22130, 2230, 11730,
        11731, 30230, 22131, 2231, 12420, 12421, 11820, 11821, 11920, 11921, 30320, 12430, 12431, 11830, 11831,
        11930, 11931, 30330,
    ),
)
ROWS = (((0,), (0,)), ((), ()))


def plane_kernel(
    pattern_ref, root_ref, panel_ref, inverse_ref, cross_ref, diag_ref,
    root, panel, inverse, own, gathered, mine, relay, acc, staged, twin_in, outer, outer_in, col, col_in,
    square, part, got, root_sem, panel_sem, inverse_sem, send_sem, recv_sem, part_send, part_recv,
):
    rows, width = panel_ref.shape
    half = width // 2
    owned = diag_ref.shape[0]
    blks = width // owned
    tile = min(rows, TILE)
    piece = rows // SUB
    sub, blk = lax.axis_index("sub"), lax.axis_index("blk")
    x, core_at, z_at, y = sub // 2, sub % 2, blk // 2, blk % 2
    level = z_at + x * (3 - 2 * z_at)
    core = core_at + x * (1 - 2 * core_at)

    def device(level_to, y_to, core_to, plane):
        return {
            "sub": plane * 2 + core_to + plane * (1 - 2 * core_to),
            "blk": (level_to + plane * (3 - 2 * level_to)) * 2 + y_to,
        }

    def here(level_to, y_to, core_to):
        return device(level_to, y_to, core_to, x)

    def there(level_to, y_to, core_to):
        return device(level_to, y_to, core_to, 1 - x)

    def twin():
        return {"sub": x * 2 + 1 - core_at}


    barrier = pltpu.get_barrier_semaphore()
    for offset in range(1, 2 * blks):
        other = lax.rem(core_at * blks + blk + offset, 2 * blks)
        pl.semaphore_signal(
            barrier, inc=1, device_id={"sub": x * 2 + other // blks, "blk": other % blks}, device_id_type=MESH
        )
    for offset in range(2):
        pl.semaphore_signal(barrier, inc=1, device_id={"sub": (1 - x) * 2 + offset}, device_id_type=MESH)

    panel_fetch = pltpu.make_async_copy(panel_ref, panel, panel_sem)
    panel_fetch.start()
    root_fetch = pltpu.make_async_copy(root_ref, root, root_sem)
    root_fetch.start()
    inverse_fetch = pltpu.make_async_copy(inverse_ref, inverse, inverse_sem)
    inverse_fetch.start()

    def at(level_of, core_of, body):
        pl.when((level == level_of) & (core == core_of))(body)

    def cut(s):
        return pl.ds(s * piece, piece)

    def copy(kind, j, s, source, target, to):
        return pltpu.make_async_remote_copy(
            src_ref=source, dst_ref=target, send_sem=send_sem.at[kind, j, s], recv_sem=recv_sem.at[kind, j, s],
            device_id=to, device_id_type=MESH,
        )

    def outgoing(level_of, core_of, kind, j, s):
        g, h = j // 2, j % 2
        far = 1 - y
        given = own.at[h, cut(s)]
        inner_near, inner_far = gathered.at[0, j, y, cut(s)], gathered.at[0, j, far, cut(s)]
        outer_near, outer_far = gathered.at[1, j, y, cut(s)], gathered.at[1, j, far, cut(s)]
        via = relay.at[h, cut(s)]
        sum_near, sum_far = col.at[j, y, cut(s)], col.at[j, far, cut(s)]
        source, target, to = {
            TWIN: lambda: (given, inner_near if level_of < 2 else mine.at[j, cut(s)], twin()),
            LIFT: lambda: (given, inner_near, here(2, y, 1)),
            UPDOWN: lambda: (given, inner_near, here(1 - level_of, y, level_of)),
            ACROSS: lambda: (given, inner_near, here(level_of, far, level_of)),
            VIA: lambda: (given, via, here(3, y, g)),
            HOP: lambda: (given, outer_near, there(3 - level_of, y, 3 - level_of)),
            HOP_SIDE_A: lambda: (outer_near, outer_near, here(0, far, core_of)),
            HOP_UP_A: lambda: (outer_near, outer_near, here(1, y, 0)),
            HOP_UP_B: lambda: (outer_far, outer_far, here(1, y, 0)),
            LIFT_A: lambda: (inner_near, inner_near, here(2, y, 0)),
            SIDE_A: lambda: (inner_near, inner_near, here(1, far, 0)),
            HOP_SIDE_B: lambda: (outer_near, outer_near, here(1, far, 1)),
            LIFT_B: lambda: (inner_far, inner_far, here(2, y, 1)),
            DROP: lambda: (inner_far, inner_far, here(0, y, 1)),
            TOP: lambda: (inner_near, inner_near, here(3, y, core_of)),
            LIFT_SIDE: lambda: (inner_near, inner_near, here(2, far, 0)),
            VIA_HOP: lambda: (via, outer_near, there(0, y, 1)),
            TOP_SIDE: lambda: (inner_near, inner_near, here(3, far, core_of)),
            BACK_A: lambda: (outer.at[j, cut(s)], outer_in.at[0, h, cut(s)], there(3 - level_of, y, g)),
            BACK_B: lambda: (outer.at[j, cut(s)], outer_in.at[1, h, cut(s)], there(3 - level_of, y, g)),
            SUM_SIDE: lambda: (sum_far, col_in.at[0, j, cut(s)], here(level_of, far, core_of)),
            SUM_B: lambda: (sum_far, col_in.at[2, j, cut(s)], here(2, y, 1)),
            SUM_A: lambda: (sum_near, col_in.at[1, j, cut(s)], here(2, y, core_of)),
            SUM_HOME: lambda: (sum_near, outer_in.at[0, h, cut(s)], here(core_of, y, g)),
            PAIR: lambda: (staged.at[j, cut(s)], twin_in.at[h, cut(s)], twin()),
        }[kind]()
        return copy(kind, j, s, source, target, to)

    def incoming(level_of, kind, j, s):
        h = j % 2
        if kind == TWIN and level_of >= 2:
            region = mine.at[j, cut(s)]
        elif kind in (TWIN, LIFT, UPDOWN, LIFT_A, TOP):
            region = gathered.at[0, j, y, cut(s)]
        elif kind in (ACROSS, SIDE_A, LIFT_SIDE, TOP_SIDE, LIFT_B, DROP):
            region = gathered.at[0, j, 1 - y, cut(s)]
        elif kind in (HOP, HOP_UP_A, VIA_HOP):
            region = gathered.at[1, j, y, cut(s)]
        elif kind in (HOP_SIDE_A, HOP_SIDE_B, HOP_UP_B):
            region = gathered.at[1, j, 1 - y, cut(s)]
        elif kind == VIA:
            region = relay.at[h, cut(s)]
        elif kind in (SUM_SIDE, SUM_A, SUM_B):
            region = col_in.at[(SUM_SIDE, SUM_A, SUM_B).index(kind), j, cut(s)]
        elif kind in (BACK_A, BACK_B):
            region = outer_in.at[kind - BACK_A, h, cut(s)]
        else:
            region = (outer_in.at[0, h, cut(s)] if kind == SUM_HOME else twin_in.at[h, cut(s)])
        return copy(kind, j, s, region, region, twin())

    def add_in(j, s, y_of, slots):
        total = col[j, y_of, cut(s)].astype(jnp.float32)
        for slot in slots:
            total += col_in[slot, j, cut(s)].astype(jnp.float32)
        col[j, y_of, cut(s)] = total.astype(jnp.bfloat16)

    def act(level_of, core_of, code):
        op, kind, j, s = code // 10000, code // 100 % 100, code // 10 % 10, code % 10
        if op == 1:
            incoming(level_of, kind, j, s).wait_recv()
        elif op == 2:
            outgoing(level_of, core_of, kind, j, s).wait_send()
        else:
            if (kind, level_of, core_of) == (SUM_A, 3, 0):
                add_in(j, s, y, (0,))
            if (kind, level_of, core_of) == (SUM_SIDE, 2, 1):
                add_in(j, s, 1 - y, (2,))
            if kind == SUM_HOME:
                add_in(j, s, y, (0, 1))
            outgoing(level_of, core_of, kind, j, s).start()

    at_code = [0] * len(PROGRAMS)

    def links(step):
        for n, program in enumerate(PROGRAMS):
            start = at_code[n]
            if step is None:
                end = len(program)
            elif step in program:
                end = program.index(step)
                at_code[n] = end + 1
            else:
                continue
            codes = program[start:end]
            if step is None:
                sent = {code for code in program if code < 10000}
                codes += tuple(sorted(20000 + code for code in sent if 20000 + code not in program))

            def body(level_of=n // 2, core_of=n % 2, codes=codes):
                for code in codes:
                    act(level_of, core_of, code)
            if codes:
                at(n // 2, n % 2, body)

    def times(q, j, at_row):
        span = pl.ds(at_row, tile)
        return jnp.dot(
            root[span, :rows], gathered[q, j, 0], preferred_element_type=jnp.float32
        ) + jnp.dot(root[span, rows:], gathered[q, j, 1], preferred_element_type=jnp.float32)

    def over_rows(body):
        @pl.loop(0, rows // tile)
        def _(step):
            body(pl.multiple_of(step * tile, tile))

    def outer_work(j):
        @pl.when(level < 2)
        def _():
            def body(at_row):
                outer[j, pl.ds(at_row, tile)] = times(1, j, at_row).astype(jnp.bfloat16)
            over_rows(body)

    def col_work(j):
        @pl.when(level >= 2)
        def _():
            for y_of in range(2):
                def body(at_row):
                    columns = pl.ds(y_of * rows + at_row, tile)
                    col[j, y_of, pl.ds(at_row, tile)] = lax.dot_general(
                        root[:, columns], mine[j], ROWS, preferred_element_type=jnp.float32
                    ).astype(jnp.bfloat16)
                over_rows(body)

    def inner_work(j):
        def body(at_row):
            span = pl.ds(at_row, tile)
            value = times(0, j, at_row)
            acc[j % 2, span] = value
            staged[j, span] = value.astype(jnp.bfloat16)
        over_rows(body)

    keeps = []
    keep_rows = min(rows, BLOCK)

    def finish(j):
        g, h = j // 2, j % 2

        @pl.when(core == g)
        def _():
            @pl.when(level < 2)
            def _():
                def body(at_row):
                    span = pl.ds(at_row, tile)
                    acc[h, span] += outer_in[0, h, span].astype(jnp.float32)
                over_rows(body)

            @pl.when(level >= 2)
            def _():
                def body(at_row):
                    span = pl.ds(at_row, tile)
                    acc[h, span] += outer_in[0, h, span].astype(jnp.float32) + outer_in[1, h, span].astype(jnp.float32)
                over_rows(body)

            for step in range(rows // tile):
                span = pl.ds(step * tile, tile)
                rounded = (acc[h, span] + twin_in[h, span].astype(jnp.float32)).astype(jnp.bfloat16)
                keep = keeps[step * tile // keep_rows]
                cross_ref[span, h * half:(h + 1) * half] = jnp.where(keep, -rounded, jnp.zeros_like(rounded))
                for a in range(h, 2):
                    square[a * half:(a + 1) * half, h * half:(h + 1) * half] += lax.dot_general(
                        own[a, span], rounded, ROWS, preferred_element_type=jnp.float32
                    )

    def part_copy(offset):
        target = lax.rem(blk + offset, blks)
        return pltpu.make_async_remote_copy(
            src_ref=part.at[target], dst_ref=got.at[offset - 1],
            send_sem=part_send.at[offset - 1], recv_sem=part_recv.at[offset - 1],
            device_id={"blk": target}, device_id_type=MESH,
        )

    def part_sends(g):
        @pl.when(core == g)
        def _():
            part[...] = square[...].astype(jnp.bfloat16).reshape(blks, owned, width)
            for offset in range(1, blks):
                part_copy(offset).start()

    panel_fetch.wait()
    for step in range(rows // keep_rows):
        keep = pattern_ref[0, (blk * rows + step * keep_rows) // BLOCK] > 0
        keeps.append(keep)
        span = pl.ds(step * keep_rows, keep_rows)
        for h in range(2):
            values = panel[span, h * half:(h + 1) * half]
            values = jnp.where(keep, values, jnp.zeros_like(values))
            own[h, span] = values

            @pl.when(level >= 2)
            def _():
                mine[2 * core + h, span] = values

            @pl.when(level == core)
            def _():
                gathered[0, 2 * core + h, y, span] = values
    inverse_fetch.wait()
    square[...] = lax.dot_general(inverse[...], inverse[...], ROWS, preferred_element_type=jnp.float32)
    root_fetch.wait()
    pl.semaphore_wait(barrier, 2 * blks + 1)
    for kind, j in STEPS:
        links(30000 + kind * 100 + j * 10)
        (col_work, outer_work, inner_work, finish)[kind](j)
        if kind == FINISH and j % 2:
            part_sends(j // 2)
    links(None)
    total = part[blk].astype(jnp.float32)
    for offset in range(1, blks):
        part_copy(offset).wait_recv()
        total += got[offset - 1].astype(jnp.float32)
    rows_at = blk * owned + lax.broadcasted_iota(jnp.int32, (owned, width), 0)
    cols_at = lax.broadcasted_iota(jnp.int32, (owned, width), 1)
    diag_ref[...] = jnp.where(cols_at <= rows_at, total, jnp.zeros_like(total))
    for offset in range(1, blks):
        part_copy(offset).wait_send()


def plane_local(blks, root_inverse, factor_panel, diag_inverse, pattern):
    rows, width = factor_panel.shape
    half = width // 2
    owned = diag_inverse.shape[0]
    dma = pltpu.SemaphoreType.DMA
    hbm = pl.BlockSpec(memory_space=pl.ANY)
    vmem = pl.BlockSpec(memory_space=pltpu.VMEM)

    def held(*lead, dtype=jnp.bfloat16):
        return pltpu.VMEM((*lead, rows, half), dtype)

    return pl.pallas_call(
        plane_kernel,
        out_shape=(
            jax.ShapeDtypeStruct((rows, width), jnp.bfloat16),
            jax.ShapeDtypeStruct((owned, width), jnp.float32),
        ),
        in_specs=[pl.BlockSpec(memory_space=pltpu.SMEM), hbm, hbm, hbm],
        out_specs=(vmem, vmem),
        scratch_shapes=[
            pltpu.VMEM(root_inverse.shape, jnp.bfloat16),
            pltpu.VMEM((rows, width), jnp.bfloat16),
            pltpu.VMEM((owned, width), jnp.bfloat16),
            held(2), held(2, 4, 2), held(4), held(2), held(2, dtype=jnp.float32), held(4), held(2),
            held(4), held(2, 2), held(4, 2), held(3, 4),
            pltpu.VMEM((width, width), jnp.float32),
            pltpu.VMEM((blks, owned, width), jnp.bfloat16),
            pltpu.VMEM((blks - 1, owned, width), jnp.bfloat16),
            dma(()), dma(()), dma(()), dma((25, 4, SUB)), dma((25, 4, SUB)), dma((blks - 1,)), dma((blks - 1,)),
        ],
        compiler_params=pltpu.CompilerParams(
            collective_id=1, has_side_effects=True, vmem_limit_bytes=60 * 1024 * 1024
        ),
    )(pattern, root_inverse, factor_panel, diag_inverse)


def fits(mesh, root_inverse, factor_panel):
    subs, blks = mesh.shape["sub"], mesh.shape["blk"]
    rows, columns = root_inverse.shape
    return (subs, blks) == (4, 8) and factor_panel.shape[1] % (4 * 256) == 0 and rows % (blks * BLOCK) == 0


def solution(mesh):
    subs, blks = mesh.shape["sub"], mesh.shape["blk"]

    def run(root_inverse, factor_panel, diag_inverse, pattern):
        body = functools.partial(local, subs, blks)
        if fits(mesh, root_inverse, factor_panel):
            body = functools.partial(plane_local, blks)
        return jax.shard_map(
            body,
            mesh=mesh,
            in_specs=(P("blk", "sub"), P("blk", "sub"), P("blk", "sub"), P("sub", None)),
            out_specs=(P("blk", "sub"), P("blk", "sub")),
            check_vma=False,
        )(root_inverse, factor_panel, diag_inverse, pattern)

    return run
```

```python
import functools

import jax
import jax.numpy as jnp
from jax import lax
from jax.experimental import pallas as pl
from jax.experimental.pallas import tpu as pltpu
from jax.sharding import PartitionSpec as P

BLOCK = 512
PANEL_CHUNKS = 2
ROOT_CHUNKS = 8
IN_FLIGHT = 3
MESH = pl.DeviceIdType.MESH


def ring_events(members, chunks):
    last = members // 2
    events = []
    for step in range(1, last + 1):
        for chunk in range(chunks):
            for way in (0, 1):
                if step < last or way == (0 if chunk < chunks // 2 else 1):
                    events.append((step, way, chunk))
    return events


def kernel(
    subs, blks, pattern_ref, root_ref, panel_ref, inverse_ref, cross_ref, diag_ref,
    root_all, panel_all, acc, panel_own, inverse_own, square, part, got,
    local_sem, panel_sem, inverse_sem, panel_send, panel_recv, root_send, root_recv,
    twin_send, twin_recv, own_twin_send, own_twin_recv, part_send, part_recv,
):
    rows, width = panel_ref.shape
    cols = root_ref.shape[1]
    ratio = cols // rows
    owned = diag_ref.shape[0]
    chips = subs // 2
    sub = lax.axis_index("sub")
    blk = lax.axis_index("blk")
    chip, core = sub // 2, sub % 2
    twin = chip * 2 + 1 - core

    half = blks // 2
    lane, side = blk // 2, blk % 2
    place = lane + side * (blks - 1 - 2 * lane)

    def blk_at(position):
        position = lax.rem(position + 2 * blks, blks)
        back = position // half
        return 2 * position + back * (2 * (blks - 1 - position) + 1 - 2 * position)

    def sub_at(position, which):
        return lax.rem(position + 2 * chips, chips) * 2 + which

    barrier = pltpu.get_barrier_semaphore()
    for offset in range(1, blks):
        pl.semaphore_signal(
            barrier, inc=1, device_id={"blk": lax.rem(blk + offset, blks)}, device_id_type=MESH
        )
    for offset in range(1, subs):
        pl.semaphore_signal(
            barrier, inc=1, device_id={"sub": lax.rem(sub + offset, subs)}, device_id_type=MESH
        )

    panel_fetch = pltpu.make_async_copy(panel_ref, panel_own, panel_sem)
    panel_fetch.start()
    local = pltpu.make_async_copy(root_ref, root_all.at[sub], local_sem)
    local.start()
    inverse_fetch = pltpu.make_async_copy(inverse_ref, inverse_own, inverse_sem)
    inverse_fetch.start()
    pl.semaphore_wait(barrier, blks - 1 + subs - 1)

    sign = (-1, 1)
    panel_rows = rows // PANEL_CHUNKS
    root_rows = rows // ROOT_CHUNKS
    sends = []

    def panel_copy(step, way, chunk, origin):
        region = panel_all.at[origin, pl.ds(chunk * panel_rows, panel_rows)]
        return pltpu.make_async_remote_copy(
            src_ref=region, dst_ref=region,
            send_sem=panel_send.at[way, step - 1, chunk],
            recv_sem=panel_recv.at[way, step - 1, chunk],
            device_id={"blk": blk_at(place - sign[way])}, device_id_type=MESH,
        )

    def root_copy(step, way, chunk, origin):
        here = pl.ds(chunk * root_rows, root_rows)
        region = root_all.at[origin, here]
        return pltpu.make_async_remote_copy(
            src_ref=root_ref.at[here] if step == 1 else region, dst_ref=region,
            send_sem=root_send.at[way, step - 1, chunk],
            recv_sem=root_recv.at[way, step - 1, chunk],
            device_id={"sub": sub_at(chip - sign[way], core)}, device_id_type=MESH,
        )

    def twin_copy(step, way, chunk, origin):
        region = root_all.at[origin, pl.ds(chunk * root_rows, root_rows)]
        return pltpu.make_async_remote_copy(
            src_ref=region, dst_ref=region,
            send_sem=twin_send.at[way, step - 1, chunk],
            recv_sem=twin_recv.at[way, step - 1, chunk],
            device_id={"sub": twin}, device_id_type=MESH,
        )

    panel_events = ring_events(blks, PANEL_CHUNKS)
    root_events = ring_events(chips, ROOT_CHUNKS)

    def send_panel(event):
        step, way, chunk = event
        if event in panel_events:
            copy = panel_copy(step, way, chunk, blk_at(place + sign[way] * (step - 1)))
            copy.start()
            sends.append(copy)

    def send_root(event):
        step, way, chunk = event
        if event in root_events:
            copy = root_copy(step, way, chunk, sub_at(chip + sign[way] * (step - 1), core))
            copy.start()
            sends.append(copy)

    first_sends = [event for event in root_events if event[0] == 1]
    for event in first_sends[:IN_FLIGHT]:
        send_root(event)
    piece_rows = min(rows, BLOCK)
    keeps = []
    panel_fetch.wait()
    for at in range(rows // piece_rows):
        keep = pattern_ref[0, (blk * rows + at * piece_rows) // BLOCK] > 0
        keeps.append(keep)
        here = pl.ds(at * piece_rows, piece_rows)
        values = panel_own[here, :]
        panel_all[blk, here, :] = jnp.where(keep, values, jnp.zeros_like(values))
    for event in panel_events:
        if event[0] == 1:
            send_panel(event)
    own_twin = pltpu.make_async_remote_copy(
        src_ref=root_ref, dst_ref=root_all.at[sub], send_sem=own_twin_send, recv_sem=own_twin_recv,
        device_id={"sub": twin}, device_id_type=MESH,
    )
    own_twin.start()
    sends.append(own_twin)

    tile = min(rows, 256)
    acc[...] = jnp.zeros_like(acc)

    def near_dot(origin):
        source = origin // ratio

        @pl.when(source // 2 == chip)
        def _():
            columns = pl.ds(pl.multiple_of((origin % ratio) * rows, rows), rows)

            @pl.loop(0, rows // tile)
            def _(at):
                here = pl.ds(pl.multiple_of(at * tile, tile), tile)
                acc[here, :] += jnp.dot(
                    root_all[source, here, columns], panel_all[origin],
                    preferred_element_type=jnp.float32,
                )

    def arrive_root(event):
        step, way, chunk = event
        origin = sub_at(chip + sign[way] * step, core)
        wait_root(event, origin)
        send_root((step + 1, way, chunk))
        if step == 1 and first_sends.index(event) + IN_FLIGHT < len(first_sends):
            send_root(first_sends[first_sends.index(event) + IN_FLIGHT])
        forward = twin_copy(step, way, chunk, origin)
        forward.start()
        sends.append(forward)

    def wait_root(event, origin):
        step, way, chunk = event
        region = root_all.at[origin, pl.ds(chunk * root_rows, root_rows)]
        pltpu.make_async_remote_copy(
            src_ref=region, dst_ref=region,
            send_sem=root_send.at[way, step - 1, chunk],
            recv_sem=root_recv.at[way, step - 1, chunk],
            device_id={"sub": sub_at(chip - sign[way], core)}, device_id_type=MESH,
        ).wait_recv()

    def arrive_panel(event):
        step, way, chunk = event
        panel_copy(step, way, chunk, blk_at(place + sign[way] * step)).wait_recv()
        send_panel((step + 1, way, chunk))

    merged = []
    for at, event in enumerate(panel_events):
        merged.append((0.87 * (at + 1) / len(panel_events), 0, event))
    for at, event in enumerate(root_events[:-2]):
        merged.append(((at + 1) / len(root_events), 1, event))
    merged.sort()

    contract_rows = (((0,), (0,)), ((), ()))
    inverse_fetch.wait()
    square[...] = lax.dot_general(
        inverse_own[...], inverse_own[...], contract_rows, preferred_element_type=jnp.float32
    )
    local.wait()
    pltpu.make_async_remote_copy(
        src_ref=root_ref, dst_ref=root_all.at[twin], send_sem=own_twin_send, recv_sem=own_twin_recv,
        device_id={"sub": twin}, device_id_type=MESH,
    ).wait_recv()
    near_dot(blk)
    for _, kind, event in merged:
        if kind == 1:
            arrive_root(event)
            continue
        arrive_panel(event)
        step, way, chunk = event
        if chunk == PANEL_CHUNKS - 1:
            if step == half:
                near_dot(blk_at(place + half))
            else:
                near_dot(blk_at(place + sign[way] * step))

    last = chips // 2

    def far_dot(events):
        step, way, chunk = events[0]
        origin = sub_at(chip + sign[way] * step, core)
        other = sub_at(chip + sign[way] * step, 1 - core)
        for event in events:
            twin_copy(*event, other).wait_recv()
        here = pl.ds(chunk * root_rows, len(events) * root_rows)
        total = acc[here, :]
        for source in (origin, other):
            for at in range(ratio):
                total += jnp.dot(
                    root_all[source, here, at * rows:(at + 1) * rows], panel_all[source * ratio + at],
                    preferred_element_type=jnp.float32,
                )
        if step < last:
            acc[here, :] = total
            return
        rounded = total.astype(jnp.bfloat16)
        keep = keeps[chunk * root_rows // piece_rows]
        cross_ref[here, :] = jnp.where(keep, -rounded, jnp.zeros_like(rounded))
        square[...] += lax.dot_general(
            panel_all[blk, here, :], rounded, contract_rows, preferred_element_type=jnp.float32
        )

    for step in range(1, last + 1):
        for way in (0, 1):
            chunks = [event for event in root_events if event[:2] == (step, way)]
            for at in range(0, len(chunks), 2):
                if (step, way, chunks[at][2]) == (last, 1, ROOT_CHUNKS - 2):
                    for event in root_events[-2:]:
                        arrive_root(event)
                        far_dot([event])
                else:
                    far_dot(chunks[at:at + 2])

    part[...] = square[...].astype(jnp.bfloat16).reshape(blks, owned, width)
    for offset in range(1, blks):
        target = lax.rem(blk + offset, blks)
        copy = pltpu.make_async_remote_copy(
            src_ref=part.at[target], dst_ref=got.at[offset - 1],
            send_sem=part_send.at[offset - 1], recv_sem=part_recv.at[offset - 1],
            device_id={"blk": target}, device_id_type=MESH,
        )
        copy.start()
        sends.append(copy)
    total = part[blk].astype(jnp.float32)
    for offset in range(1, blks):
        sends[offset - blks].wait_recv()
        total += got[offset - 1].astype(jnp.float32)
    rows_at = blk * owned + lax.broadcasted_iota(jnp.int32, (owned, width), 0)
    cols_at = lax.broadcasted_iota(jnp.int32, (owned, width), 1)
    diag_ref[...] = jnp.where(cols_at <= rows_at, total, jnp.zeros_like(total))
    for copy in sends:
        copy.wait_send()


def local(subs, blks, root_inverse, factor_panel, diag_inverse, pattern):
    rows, width = factor_panel.shape
    cols = root_inverse.shape[1]
    owned = diag_inverse.shape[0]
    dma = pltpu.SemaphoreType.DMA
    panel_sems = dma((2, blks // 2, PANEL_CHUNKS))
    root_sems = dma((2, subs // 4, ROOT_CHUNKS))
    hbm = pl.BlockSpec(memory_space=pl.ANY)
    vmem = pl.BlockSpec(memory_space=pltpu.VMEM)
    return pl.pallas_call(
        functools.partial(kernel, subs, blks),
        out_shape=(
            jax.ShapeDtypeStruct((rows, width), jnp.bfloat16),
            jax.ShapeDtypeStruct((owned, width), jnp.float32),
        ),
        in_specs=[
            pl.BlockSpec(memory_space=pltpu.SMEM), hbm, hbm, hbm,
        ],
        out_specs=(vmem, vmem),
        scratch_shapes=[
            pltpu.VMEM((subs, rows, cols), jnp.bfloat16),
            pltpu.VMEM((blks, rows, width), jnp.bfloat16),
            pltpu.VMEM((rows, width), jnp.float32),
            pltpu.VMEM((rows, width), jnp.bfloat16),
            pltpu.VMEM((owned, width), jnp.bfloat16),
            pltpu.VMEM((width, width), jnp.float32),
            pltpu.VMEM((blks, owned, width), jnp.bfloat16),
            pltpu.VMEM((blks - 1, owned, width), jnp.bfloat16),
            dma(()), dma(()), dma(()), panel_sems, panel_sems, root_sems, root_sems, root_sems, root_sems, dma(()), dma(()),
            dma((blks - 1,)), dma((blks - 1,)),
        ],
        compiler_params=pltpu.CompilerParams(
            collective_id=0, has_side_effects=True, vmem_limit_bytes=60 * 1024 * 1024
        ),
    )(pattern, root_inverse, factor_panel, diag_inverse)


SUB = 2
TILE = 256
(
    TWIN, LIFT, UPDOWN, ACROSS, VIA, HOP, HOP_SIDE_A, HOP_UP_A, HOP_UP_B, LIFT_A, SIDE_A, HOP_SIDE_B, LIFT_B, DROP, TOP,
    LIFT_SIDE, VIA_HOP, TOP_SIDE, BACK_A, BACK_B, SUM_SIDE, SUM_B, SUM_A, SUM_HOME, PAIR,
) = range(25)
COL, OUTER, INNER, FINISH, BEGIN = range(5)
STEPS = (
    (BEGIN, 0), (COL, 0), (COL, 1), (COL, 2), (COL, 3), (OUTER, 0), (INNER, 0), (OUTER, 1), (INNER, 1), (FINISH, 0),
    (OUTER, 2), (INNER, 2), (FINISH, 1), (OUTER, 3), (INNER, 3), (FINISH, 2), (FINISH, 3),
)
PROGRAMS = (
    (
        30400, 300, 301, 200, 201, 20200, 210, 20300, 310, 20201, 211, 10500, 20301, 600, 20210, 700, 20310,
        311, 10501, 20600, 601, 20211, 701, 10510, 20311, 610, 20700, 710, 10511, 20601, 611, 20701, 711,
        10600, 20710, 800, 10601, 20711, 801, 30100, 1800, 1801, 10300, 10301, 30200, 10610, 10611, 30110,
        21800, 1810, 21801, 1811, 10310, 10311, 30210, 10520, 20610, 620, 20800, 810, 10521, 20611, 621, 20801,
        811, 20810, 720, 20811, 721, 10530, 20620, 630, 10620, 20720, 820, 10621, 20721, 821, 12400, 12401,
        12300, 12301, 30300, 10531, 20621, 631, 30120, 21810, 1820, 21811, 1821, 10320, 10321, 10020, 10021,
        30220, 2420, 2421, 12410, 12411, 12310, 12311, 30310, 20820, 730, 20821, 731, 10630, 10631, 30130,
        21820, 1830, 21821, 1831, 20730, 830, 20731, 831, 10330, 10331, 10030, 10031, 30230, 2430, 2431,
    ),
    (
        30400, 30, 31, 20, 21, 11600, 600, 11601, 601, 220, 221, 11610, 20600, 610, 11611, 20601, 611, 20610,
        320, 10600, 10601, 30100, 1900, 1901, 10200, 10201, 11300, 11301, 30200, 2400, 2401, 10610, 10611,
        30110, 21900, 1910, 21901, 1911, 10210, 10211, 11310, 11311, 30210, 2410, 2411, 20611, 330, 20320, 321,
        20220, 230, 11620, 20330, 620, 20221, 231, 20321, 331, 11621, 20620, 621, 11630, 20331, 630, 11631,
        20621, 631, 10620, 10621, 30120, 21910, 1920, 21911, 1921, 10220, 10221, 11320, 11321, 30220, 10630,
        10631, 30130, 21920, 1930, 21921, 1931, 10230, 10231, 11330, 11331, 30230, 12420, 12421, 12320, 12321,
        30320, 12430, 12431, 12330, 12331, 30330,
    ),
    (
        30400, 300, 100, 301, 101, 0, 1, 210, 211, 20300, 310, 20301, 311, 10, 11, 20210, 200, 20211, 201,
        20100, 110, 10200, 20101, 900, 20110, 111, 10201, 20900, 901, 20310, 1000, 20311, 1001, 10210, 20111,
        910, 10211, 20901, 911, 21000, 1010, 21001, 1011, 10700, 10701, 10800, 10801, 30100, 1800, 1801, 11000,
        11001, 30200, 10710, 10711, 10810, 10811, 30110, 11010, 11011, 30210, 12400, 12401, 12300, 12301,
        30300, 10220, 20910, 920, 21010, 1020, 10221, 20911, 921, 21011, 1021, 10230, 20920, 930, 21800, 1810,
        10231, 20921, 931, 21801, 1811, 10720, 10721, 10820, 10821, 30120, 21810, 1820, 21811, 1821, 11020,
        11021, 30220, 12410, 12411, 12310, 12311, 30310, 21020, 1030, 2420, 2421, 21021, 1031, 10730, 10731,
        10830, 10831, 30130, 21820, 1830, 21821, 1831, 11030, 11031, 30230, 2430, 2431,
    ),
    (
        30400, 10500, 1100, 10501, 1101, 10300, 1300, 10301, 1301, 10310, 21300, 1310, 10311, 21301, 1311,
        1200, 21310, 220, 11100, 11101, 30100, 1900, 1901, 1201, 21311, 221, 21200, 120, 10510, 21100, 1110,
        21201, 121, 10511, 21101, 1111, 10520, 21110, 1120, 20220, 230, 20120, 1210, 21111, 320, 10000, 10001,
        30200, 2400, 2401, 20121, 1211, 10521, 21120, 1121, 20221, 231, 11110, 11111, 30110, 10010, 10011,
        30210, 2410, 2411, 21210, 130, 20320, 321, 21211, 131, 21900, 1910, 10530, 21121, 1130, 21901, 1911,
        11120, 11121, 30120, 21910, 1920, 21911, 1921, 10320, 20230, 1320, 20321, 330, 10531, 21130, 1131,
        20130, 1220, 10321, 20231, 1321, 20131, 1221, 20330, 331, 10330, 21320, 1330, 21220, 1230, 10331,
        21221, 1231, 21321, 1331, 30220, 11130, 11131, 30130, 21920, 1930, 21921, 1931, 30230, 12420, 12421,
        12320, 12321, 30320, 12430, 12431, 12330, 12331, 30330,
    ),
    (
        30400, 10, 11, 400, 0, 401, 1, 500, 501, 30000, 2000, 2001, 20500, 510, 30010, 22000, 2010, 22001,
        2011, 20400, 410, 20501, 511, 10020, 10021, 30020, 10030, 10031, 30030, 20401, 411, 10900, 22010, 1500,
        22011, 2020, 10901, 21500, 1501, 22020, 2021, 12200, 12000, 2300, 20410, 1400, 12201, 12001, 2301,
        20411, 1401, 11500, 11501, 30200, 10910, 21400, 1410, 21501, 1510, 22021, 2030, 10911, 21401, 1411,
        21510, 1511, 22030, 2031, 12210, 12010, 22300, 2310, 12211, 12011, 22301, 2311, 12220, 12020, 22310,
        2320, 10920, 21511, 1520, 21410, 1420, 10921, 22031, 1521, 11510, 11511, 30210, 12400, 12401, 11800,
        11801, 11900, 11901, 30300, 21411, 1421, 12221, 12021, 22311, 2321, 10930, 21420, 1430, 12230, 12030,
        22320, 2330, 21520, 1530, 10931, 21421, 1431, 21521, 1531, 12231, 12031, 22321, 2331, 11520, 11521,
        30220, 2420, 2421, 12410, 12411, 11810, 11811, 11910, 11911, 30310, 11530, 11531, 30230, 2430, 2431,
    ),
    (
        30400, 20, 21, 30, 31, 10000, 10001, 30000, 10100, 1400, 10010, 10011, 30010, 30020, 10101, 1401, 520,
        10110, 21400, 1410, 521, 12100, 2000, 10111, 21401, 1411, 30030, 12101, 2001, 20520, 530, 20521, 531,
        12200, 12000, 2300, 21410, 420, 12201, 12001, 2301, 21411, 421, 12110, 22000, 2010, 12111, 22001, 2011,
        20420, 430, 10120, 20421, 1420, 20430, 431, 10121, 21420, 1421, 12210, 12010, 22300, 2310, 10130,
        20431, 1430, 12211, 12011, 22301, 2311, 12120, 22010, 2020, 11200, 11201, 30200, 2400, 2401, 11210,
        11211, 30210, 2410, 2411, 12220, 12020, 22310, 2320, 10131, 21421, 1431, 12121, 22011, 2021, 12130,
        22020, 2030, 12221, 12021, 22311, 2321, 12131, 22021, 2031, 11220, 11221, 30220, 12230, 12030, 22320,
        2330, 11230, 11231, 30230, 12231, 12031, 22321, 2331, 12420, 12421, 11820, 11821, 11920, 11921, 30320,
        12430, 12431, 11830, 11831, 11930, 11931, 30330,
    ),
    (
        30400, 500, 501, 10, 11, 0, 1, 30000, 2000, 2001, 30010, 10020, 10021, 30020, 22000, 2020, 22001, 2021,
        20500, 510, 20501, 511, 22020, 2010, 10400, 20510, 1600, 12000, 2200, 10030, 10031, 30030, 22021, 2011,
        10401, 20511, 1601, 22010, 2030, 12001, 2201, 10410, 21600, 1610, 12010, 22200, 2210, 10411, 21601,
        1611, 12011, 22201, 2211, 22011, 2031, 11400, 22030, 1700, 11401, 22031, 1701, 11700, 11701, 30200,
        11410, 21700, 1710, 11411, 21701, 1711, 12020, 22210, 2220, 12021, 22211, 2221, 12030, 22220, 2230,
        11420, 21710, 1720, 11710, 11711, 30210, 12400, 12401, 11800, 11801, 11900, 11901, 30300, 11421, 21711,
        1721, 12031, 22221, 2231, 11430, 21720, 1730, 11431, 21721, 1731, 11720, 11721, 30220, 2420, 2421,
        12410, 12411, 11810, 11811, 11910, 11911, 30310, 11730, 11731, 30230, 2430, 2431,
    ),
    (
        30400, 30, 31, 20, 21, 10000, 10001, 30000, 2100, 10010, 10011, 30010, 2101, 22100, 2200, 30020, 22101,
        2201, 22200, 2110, 22201, 2111, 30030, 22110, 2210, 520, 11410, 1710, 521, 22111, 2211, 22210, 2220,
        11411, 1711, 20520, 530, 11400, 21710, 1700, 22211, 2120, 20521, 531, 11401, 21711, 1701, 22220, 2121,
        22120, 2221, 10420, 20530, 1620, 10421, 20531, 1621, 11420, 21700, 1720, 11421, 21701, 1721, 22121,
        2130, 11700, 11701, 30200, 2400, 2401, 11710, 11711, 30210, 2410, 2411, 10430, 21620, 1630, 22221,
        2131, 10431, 21621, 1631, 11430, 21720, 1730, 11431, 21721, 1731, 11720, 11721, 30220, 22130, 2230,
        11730, 11731, 30230, 22131, 2231, 12420, 12421, 11820, 11821, 11920, 11921, 30320, 12430, 12431, 11830,
        11831, 11930, 11931, 30330,
    ),
)
ROWS = (((0,), (0,)), ((), ()))


def plane_kernel(
    pattern_ref, root_ref, panel_ref, inverse_ref, cross_ref, diag_ref,
    root, panel, inverse, cross, own, gathered, mine, relay, acc, staged, twin_in, outer, outer_in, col, col_in,
    square, part, got, root_sem, panel_sem, inverse_sem, cross_sem, send_sem, recv_sem, part_send, part_recv,
):
    rows, width = panel_ref.shape
    half = width // 2
    owned = diag_ref.shape[0]
    blks = width // owned
    tile = min(rows, TILE)
    piece = rows // SUB
    sub, blk = lax.axis_index("sub"), lax.axis_index("blk")
    x, core_at, z_at, y = sub // 2, sub % 2, blk // 2, blk % 2
    level = z_at + x * (3 - 2 * z_at)
    core = core_at + x * (1 - 2 * core_at)

    def device(level_to, y_to, core_to, plane):
        return {
            "sub": plane * 2 + core_to + plane * (1 - 2 * core_to),
            "blk": (level_to + plane * (3 - 2 * level_to)) * 2 + y_to,
        }

    def here(level_to, y_to, core_to):
        return device(level_to, y_to, core_to, x)

    def there(level_to, y_to, core_to):
        return device(level_to, y_to, core_to, 1 - x)

    def twin():
        return {"sub": x * 2 + 1 - core_at}


    barrier = pltpu.get_barrier_semaphore()
    for offset in range(1, 2 * blks):
        other = lax.rem(core_at * blks + blk + offset, 2 * blks)
        pl.semaphore_signal(
            barrier, inc=1, device_id={"sub": x * 2 + other // blks, "blk": other % blks}, device_id_type=MESH
        )
    for offset in range(2):
        pl.semaphore_signal(barrier, inc=1, device_id={"sub": (1 - x) * 2 + offset}, device_id_type=MESH)

    def halves(ref, h):
        return ref.at[:, pl.ds(h * half, half)]

    panel_fetch = pltpu.make_async_copy(panel_ref, panel, panel_sem)
    panel_fetch.start()
    root_fetch = pltpu.make_async_copy(root_ref, root, root_sem)
    root_fetch.start()
    inverse_fetch = pltpu.make_async_copy(inverse_ref, inverse, inverse_sem)
    inverse_fetch.start()

    def at(level_of, core_of, body):
        pl.when((level == level_of) & (core == core_of))(body)

    def cut(s):
        return pl.ds(s * piece, piece)

    def copy(kind, j, s, source, target, to):
        return pltpu.make_async_remote_copy(
            src_ref=source, dst_ref=target, send_sem=send_sem.at[kind, j, s], recv_sem=recv_sem.at[kind, j, s],
            device_id=to, device_id_type=MESH,
        )

    def outgoing(level_of, core_of, kind, j, s):
        g, h = j // 2, j % 2
        far = 1 - y
        given = own.at[h, cut(s)]
        inner_near, inner_far = gathered.at[0, j, y, cut(s)], gathered.at[0, j, far, cut(s)]
        outer_near, outer_far = gathered.at[1, j, y, cut(s)], gathered.at[1, j, far, cut(s)]
        via = relay.at[h, cut(s)]
        sum_near, sum_far = col.at[j, y, cut(s)], col.at[j, far, cut(s)]
        source, target, to = {
            TWIN: lambda: (given, inner_near if level_of < 2 else mine.at[j, cut(s)], twin()),
            LIFT: lambda: (given, inner_near, here(2, y, 1)),
            UPDOWN: lambda: (given, inner_near, here(1 - level_of, y, level_of)),
            ACROSS: lambda: (given, inner_near, here(level_of, far, level_of)),
            VIA: lambda: (given, via, here(3, y, g)),
            HOP: lambda: (given, outer_near, there(3 - level_of, y, 3 - level_of)),
            HOP_SIDE_A: lambda: (outer_near, outer_near, here(0, far, core_of)),
            HOP_UP_A: lambda: (outer_near, outer_near, here(1, y, 0)),
            HOP_UP_B: lambda: (outer_far, outer_far, here(1, y, 0)),
            LIFT_A: lambda: (inner_near, inner_near, here(2, y, 0)),
            SIDE_A: lambda: (inner_near, inner_near, here(1, far, 0)),
            HOP_SIDE_B: lambda: (outer_near, outer_near, here(1, far, 1)),
            LIFT_B: lambda: (inner_far, inner_far, here(2, y, 1)),
            DROP: lambda: (inner_far, inner_far, here(0, y, 1)),
            TOP: lambda: (inner_near, inner_near, here(3, y, core_of)),
            LIFT_SIDE: lambda: (inner_near, inner_near, here(2, far, 0)),
            VIA_HOP: lambda: (via, outer_near, there(0, y, 1)),
            TOP_SIDE: lambda: (inner_near, inner_near, here(3, far, core_of)),
            BACK_A: lambda: (outer.at[j, cut(s)], outer_in.at[0, h, cut(s)], there(3 - level_of, y, g)),
            BACK_B: lambda: (outer.at[j, cut(s)], outer_in.at[1, h, cut(s)], there(3 - level_of, y, g)),
            SUM_SIDE: lambda: (sum_far, col_in.at[0, j, cut(s)], here(level_of, far, core_of)),
            SUM_B: lambda: (sum_far, col_in.at[2, j, cut(s)], here(2, y, 1)),
            SUM_A: lambda: (sum_near, col_in.at[1, j, cut(s)], here(2, y, core_of)),
            SUM_HOME: lambda: (sum_near, outer_in.at[0, h, cut(s)], here(core_of, y, g)),
            PAIR: lambda: (staged.at[j, cut(s)], twin_in.at[h, cut(s)], twin()),
        }[kind]()
        return copy(kind, j, s, source, target, to)

    def incoming(level_of, kind, j, s):
        h = j % 2
        if kind == TWIN and level_of >= 2:
            region = mine.at[j, cut(s)]
        elif kind in (TWIN, LIFT, UPDOWN, LIFT_A, TOP):
            region = gathered.at[0, j, y, cut(s)]
        elif kind in (ACROSS, SIDE_A, LIFT_SIDE, TOP_SIDE, LIFT_B, DROP):
            region = gathered.at[0, j, 1 - y, cut(s)]
        elif kind in (HOP, HOP_UP_A, VIA_HOP):
            region = gathered.at[1, j, y, cut(s)]
        elif kind in (HOP_SIDE_A, HOP_SIDE_B, HOP_UP_B):
            region = gathered.at[1, j, 1 - y, cut(s)]
        elif kind == VIA:
            region = relay.at[h, cut(s)]
        elif kind in (SUM_SIDE, SUM_A, SUM_B):
            region = col_in.at[(SUM_SIDE, SUM_A, SUM_B).index(kind), j, cut(s)]
        elif kind in (BACK_A, BACK_B):
            region = outer_in.at[kind - BACK_A, h, cut(s)]
        else:
            region = (outer_in.at[0, h, cut(s)] if kind == SUM_HOME else twin_in.at[h, cut(s)])
        return copy(kind, j, s, region, region, twin())

    def add_in(j, s, y_of, slots):
        total = col[j, y_of, cut(s)].astype(jnp.float32)
        for slot in slots:
            total += col_in[slot, j, cut(s)].astype(jnp.float32)
        col[j, y_of, cut(s)] = total.astype(jnp.bfloat16)

    def act(level_of, core_of, code):
        op, kind, j, s = code // 10000, code // 100 % 100, code // 10 % 10, code % 10
        if op == 1:
            incoming(level_of, kind, j, s).wait_recv()
        elif op == 2:
            outgoing(level_of, core_of, kind, j, s).wait_send()
        else:
            if (kind, level_of, core_of) == (SUM_A, 3, 0):
                add_in(j, s, y, (0,))
            if (kind, level_of, core_of) == (SUM_SIDE, 2, 1):
                add_in(j, s, 1 - y, (2,))
            if kind == SUM_HOME:
                add_in(j, s, y, (0, 1))
            outgoing(level_of, core_of, kind, j, s).start()

    at_code = [0] * len(PROGRAMS)

    def links(step):
        for n, program in enumerate(PROGRAMS):
            start = at_code[n]
            if step is None:
                end = len(program)
            elif step in program:
                end = program.index(step)
                at_code[n] = end + 1
            else:
                continue
            codes = program[start:end]
            if step is None:
                sent = {code for code in program if code < 10000}
                codes += tuple(sorted(20000 + code for code in sent if 20000 + code not in program))

            def body(level_of=n // 2, core_of=n % 2, codes=codes):
                for code in codes:
                    act(level_of, core_of, code)
            if codes:
                at(n // 2, n % 2, body)

    def times(q, j, at_row):
        span = pl.ds(at_row, tile)
        return jnp.dot(
            root[span, :rows], gathered[q, j, 0], preferred_element_type=jnp.float32
        ) + jnp.dot(root[span, rows:], gathered[q, j, 1], preferred_element_type=jnp.float32)

    def over_rows(body):
        @pl.loop(0, rows // tile)
        def _(step):
            body(pl.multiple_of(step * tile, tile))

    def outer_work(j):
        @pl.when(level < 2)
        def _():
            def body(at_row):
                outer[j, pl.ds(at_row, tile)] = times(1, j, at_row).astype(jnp.bfloat16)
            over_rows(body)

    def col_work(j):
        @pl.when(level >= 2)
        def _():
            for y_of in range(2):
                def body(at_row):
                    columns = pl.ds(y_of * rows + at_row, tile)
                    col[j, y_of, pl.ds(at_row, tile)] = lax.dot_general(
                        root[:, columns], mine[j], ROWS, preferred_element_type=jnp.float32
                    ).astype(jnp.bfloat16)
                over_rows(body)

    def inner_work(j):
        def body(at_row):
            span = pl.ds(at_row, tile)
            value = times(0, j, at_row)
            acc[j, span] = value
            staged[j, span] = value.astype(jnp.bfloat16)
        over_rows(body)

    keep_rows = min(rows, BLOCK)

    def finish(j):
        g, h = j // 2, j % 2

        @pl.when(core == g)
        def _():
            @pl.when(level < 2)
            def _():
                def body(at_row):
                    span = pl.ds(at_row, tile)
                    acc[j, span] += outer_in[0, h, span].astype(jnp.float32)
                over_rows(body)

            @pl.when(level >= 2)
            def _():
                def body(at_row):
                    span = pl.ds(at_row, tile)
                    acc[j, span] += outer_in[0, h, span].astype(jnp.float32) + outer_in[1, h, span].astype(jnp.float32)
                over_rows(body)

            for step in range(rows // tile):
                span = pl.ds(step * tile, tile)
                rounded = (acc[j, span] + twin_in[h, span].astype(jnp.float32)).astype(jnp.bfloat16)
                keep = keeps[step * tile // keep_rows]
                cross[h, span] = jnp.where(keep, -rounded, jnp.zeros_like(rounded))
                for a in range(h, 2):
                    square[a * half:(a + 1) * half, h * half:(h + 1) * half] += lax.dot_general(
                        own[a, span], rounded, ROWS, preferred_element_type=jnp.float32
                    )

    def cross_store(h):
        return pltpu.make_async_copy(cross.at[h], halves(cross_ref, h), cross_sem.at[h])

    def first_owner(h):
        return h * (blks // 2)

    def wide(h, owner):
        lanes = min(half, 128)
        return min(half, -((h * half - (owner + 1) * owned) // lanes) * lanes)

    def part_copy(h, sender, owner, to):
        columns = pl.ds(0, wide(h, owner))
        return pltpu.make_async_remote_copy(
            src_ref=part.at[h, owner, :, columns], dst_ref=got.at[h, sender, :, columns],
            send_sem=part_send.at[h, owner], recv_sem=part_recv.at[h, sender],
            device_id={"blk": to}, device_id_type=MESH,
        )

    def part_sends(j):
        h = j % 2

        @pl.when(core == j // 2)
        def _():
            first = first_owner(h)
            lower = square[first * owned:, h * half:(h + 1) * half]
            part[h, first:] = lower.astype(jnp.bfloat16).reshape(blks - first, owned, half)
            for owner in reversed(range(first, blks)):
                @pl.when(owner != blk)
                def _():
                    part_copy(h, blk, owner, owner).start()
            cross_store(h).start()

    def part_sum(h, owner):
        @pl.when(blk == owner)
        def _():
            columns = wide(h, owner)
            total = part[h, owner, :, :columns].astype(jnp.float32)
            for sender in range(blks):
                if sender != owner:
                    part_copy(h, sender, owner, sender).wait_recv()
                    total += got[h, sender, :, :columns].astype(jnp.float32)
            rows_at = owner * owned + lax.broadcasted_iota(jnp.int32, (owned, columns), 0)
            cols_at = h * half + lax.broadcasted_iota(jnp.int32, (owned, columns), 1)
            diag_ref[:, h * half:h * half + columns] = jnp.where(cols_at <= rows_at, total, jnp.zeros_like(total))

    keeps = [pattern_ref[0, (blk * rows + step * keep_rows) // BLOCK] > 0 for step in range(rows // keep_rows)]

    def mask(h):
        for step, keep in enumerate(keeps):
            span = pl.ds(step * keep_rows, keep_rows)
            values = panel[span, h * half:(h + 1) * half]
            values = jnp.where(keep, values, jnp.zeros_like(values))
            own[h, span] = values

            @pl.when(level >= 2)
            def _():
                mine[2 * core + h, span] = values

            @pl.when(level == core)
            def _():
                gathered[0, 2 * core + h, y, span] = values

    def begin(_):
        mask(1)
        inverse_fetch.wait()
        square[...] = lax.dot_general(inverse[...], inverse[...], ROWS, preferred_element_type=jnp.float32)
        diag_ref[...] = jnp.zeros_like(diag_ref)
        root_fetch.wait()

    panel_fetch.wait()
    mask(0)
    pl.semaphore_wait(barrier, 2 * blks + 1)
    for kind, j in STEPS:
        links(30000 + kind * 100 + j * 10)
        (col_work, outer_work, inner_work, finish, begin)[kind](j)
        if kind == FINISH:
            part_sends(j)
    for h in range(2):
        for owner in range(first_owner(h), blks):
            part_sum(h, owner)
    links(None)
    for h in range(2):
        cross_store(h).wait()
        for owner in range(first_owner(h), blks):
            @pl.when(blk != owner)
            def _():
                part_copy(h, blk, owner, owner).wait_send()


def hand_on(cross_in, diag_in, cross_out, diag_out):
    cross_out[...] = cross_in[...]
    diag_out[...] = diag_in[...]


def plane_local(blks, root_inverse, factor_panel, diag_inverse, pattern):
    rows, width = factor_panel.shape
    half = width // 2
    owned = diag_inverse.shape[0]
    dma = pltpu.SemaphoreType.DMA
    hbm = pl.BlockSpec(memory_space=pl.ANY)
    vmem = pl.BlockSpec(memory_space=pltpu.VMEM)

    def held(*lead, dtype=jnp.bfloat16):
        return pltpu.VMEM((*lead, rows, half), dtype)

    cross, diag = pl.pallas_call(
        plane_kernel,
        out_shape=(
            jax.ShapeDtypeStruct((rows, width), jnp.bfloat16),
            jax.ShapeDtypeStruct((owned, width), jnp.float32),
        ),
        in_specs=[pl.BlockSpec(memory_space=pltpu.SMEM), hbm, hbm, hbm],
        out_specs=(hbm, vmem),
        scratch_shapes=[
            pltpu.VMEM(root_inverse.shape, jnp.bfloat16),
            pltpu.VMEM((rows, width), jnp.bfloat16),
            pltpu.VMEM((owned, width), jnp.bfloat16),
            held(2), held(2), held(2, 4, 2), held(4), held(2), held(4, dtype=jnp.float32), held(4), held(2),
            held(4), held(2, 2), held(4, 2), held(3, 4),
            pltpu.VMEM((width, width), jnp.float32),
            pltpu.VMEM((2, blks, owned, half), jnp.bfloat16),
            pltpu.VMEM((2, blks, owned, half), jnp.bfloat16),
            dma(()), dma(()), dma(()), dma((2,)), dma((25, 4, SUB)), dma((25, 4, SUB)), dma((2, blks)), dma((2, blks)),
        ],
        compiler_params=pltpu.CompilerParams(
            collective_id=1, has_side_effects=True, vmem_limit_bytes=60 * 1024 * 1024
        ),
    )(pattern, root_inverse, factor_panel, diag_inverse)
    return pl.pallas_call(
        hand_on,
        out_shape=(jax.ShapeDtypeStruct(cross.shape, cross.dtype), jax.ShapeDtypeStruct(diag.shape, diag.dtype)),
        in_specs=[vmem, vmem],
        out_specs=(vmem, vmem),
    )(cross, diag)


def fits(mesh, root_inverse, factor_panel):
    subs, blks = mesh.shape["sub"], mesh.shape["blk"]
    rows, columns = root_inverse.shape
    return (subs, blks) == (4, 8) and factor_panel.shape[1] % (4 * 256) == 0 and rows % (blks * BLOCK) == 0


def solution(mesh):
    subs, blks = mesh.shape["sub"], mesh.shape["blk"]

    def run(root_inverse, factor_panel, diag_inverse, pattern):
        body = functools.partial(local, subs, blks)
        if fits(mesh, root_inverse, factor_panel):
            body = functools.partial(plane_local, blks)
        return jax.shard_map(
            body,
            mesh=mesh,
            in_specs=(P("blk", "sub"), P("blk", "sub"), P("blk", "sub"), P("sub", None)),
            out_specs=(P("blk", "sub"), P("blk", "sub")),
            check_vma=False,
        )(root_inverse, factor_panel, diag_inverse, pattern)

    return run
```

```python
import functools

import jax
import jax.numpy as jnp
from jax import lax
from jax.experimental import pallas as pl
from jax.experimental.pallas import tpu as pltpu
from jax.sharding import PartitionSpec as P

BLOCK = 512
PANEL_CHUNKS = 2
ROOT_CHUNKS = 8
IN_FLIGHT = 3
MESH = pl.DeviceIdType.MESH


def ring_events(members, chunks):
    last = members // 2
    events = []
    for step in range(1, last + 1):
        for chunk in range(chunks):
            for way in (0, 1):
                if step < last or way == (0 if chunk < chunks // 2 else 1):
                    events.append((step, way, chunk))
    return events


def kernel(
    subs, blks, pattern_ref, root_ref, panel_ref, inverse_ref, cross_ref, diag_ref,
    root_all, panel_all, acc, panel_own, inverse_own, square, part, got,
    local_sem, panel_sem, inverse_sem, panel_send, panel_recv, root_send, root_recv,
    twin_send, twin_recv, own_twin_send, own_twin_recv, part_send, part_recv,
):
    rows, width = panel_ref.shape
    cols = root_ref.shape[1]
    ratio = cols // rows
    owned = diag_ref.shape[0]
    chips = subs // 2
    sub = lax.axis_index("sub")
    blk = lax.axis_index("blk")
    chip, core = sub // 2, sub % 2
    twin = chip * 2 + 1 - core

    half = blks // 2
    lane, side = blk // 2, blk % 2
    place = lane + side * (blks - 1 - 2 * lane)

    def blk_at(position):
        position = lax.rem(position + 2 * blks, blks)
        back = position // half
        return 2 * position + back * (2 * (blks - 1 - position) + 1 - 2 * position)

    def sub_at(position, which):
        return lax.rem(position + 2 * chips, chips) * 2 + which

    barrier = pltpu.get_barrier_semaphore()
    for offset in range(1, blks):
        pl.semaphore_signal(
            barrier, inc=1, device_id={"blk": lax.rem(blk + offset, blks)}, device_id_type=MESH
        )
    for offset in range(1, subs):
        pl.semaphore_signal(
            barrier, inc=1, device_id={"sub": lax.rem(sub + offset, subs)}, device_id_type=MESH
        )

    panel_fetch = pltpu.make_async_copy(panel_ref, panel_own, panel_sem)
    panel_fetch.start()
    local = pltpu.make_async_copy(root_ref, root_all.at[sub], local_sem)
    local.start()
    inverse_fetch = pltpu.make_async_copy(inverse_ref, inverse_own, inverse_sem)
    inverse_fetch.start()
    pl.semaphore_wait(barrier, blks - 1 + subs - 1)

    sign = (-1, 1)
    panel_rows = rows // PANEL_CHUNKS
    root_rows = rows // ROOT_CHUNKS
    sends = []

    def panel_copy(step, way, chunk, origin):
        region = panel_all.at[origin, pl.ds(chunk * panel_rows, panel_rows)]
        return pltpu.make_async_remote_copy(
            src_ref=region, dst_ref=region,
            send_sem=panel_send.at[way, step - 1, chunk],
            recv_sem=panel_recv.at[way, step - 1, chunk],
            device_id={"blk": blk_at(place - sign[way])}, device_id_type=MESH,
        )

    def root_copy(step, way, chunk, origin):
        here = pl.ds(chunk * root_rows, root_rows)
        region = root_all.at[origin, here]
        return pltpu.make_async_remote_copy(
            src_ref=root_ref.at[here] if step == 1 else region, dst_ref=region,
            send_sem=root_send.at[way, step - 1, chunk],
            recv_sem=root_recv.at[way, step - 1, chunk],
            device_id={"sub": sub_at(chip - sign[way], core)}, device_id_type=MESH,
        )

    def twin_copy(step, way, chunk, origin):
        region = root_all.at[origin, pl.ds(chunk * root_rows, root_rows)]
        return pltpu.make_async_remote_copy(
            src_ref=region, dst_ref=region,
            send_sem=twin_send.at[way, step - 1, chunk],
            recv_sem=twin_recv.at[way, step - 1, chunk],
            device_id={"sub": twin}, device_id_type=MESH,
        )

    panel_events = ring_events(blks, PANEL_CHUNKS)
    root_events = ring_events(chips, ROOT_CHUNKS)

    def send_panel(event):
        step, way, chunk = event
        if event in panel_events:
            copy = panel_copy(step, way, chunk, blk_at(place + sign[way] * (step - 1)))
            copy.start()
            sends.append(copy)

    def send_root(event):
        step, way, chunk = event
        if event in root_events:
            copy = root_copy(step, way, chunk, sub_at(chip + sign[way] * (step - 1), core))
            copy.start()
            sends.append(copy)

    first_sends = [event for event in root_events if event[0] == 1]
    for event in first_sends[:IN_FLIGHT]:
        send_root(event)
    piece_rows = min(rows, BLOCK)
    keeps = []
    panel_fetch.wait()
    for at in range(rows // piece_rows):
        keep = pattern_ref[0, (blk * rows + at * piece_rows) // BLOCK] > 0
        keeps.append(keep)
        here = pl.ds(at * piece_rows, piece_rows)
        values = panel_own[here, :]
        panel_all[blk, here, :] = jnp.where(keep, values, jnp.zeros_like(values))
    for event in panel_events:
        if event[0] == 1:
            send_panel(event)
    own_twin = pltpu.make_async_remote_copy(
        src_ref=root_ref, dst_ref=root_all.at[sub], send_sem=own_twin_send, recv_sem=own_twin_recv,
        device_id={"sub": twin}, device_id_type=MESH,
    )
    own_twin.start()
    sends.append(own_twin)

    tile = min(rows, 256)
    acc[...] = jnp.zeros_like(acc)

    def near_dot(origin):
        source = origin // ratio

        @pl.when(source // 2 == chip)
        def _():
            columns = pl.ds(pl.multiple_of((origin % ratio) * rows, rows), rows)

            @pl.loop(0, rows // tile)
            def _(at):
                here = pl.ds(pl.multiple_of(at * tile, tile), tile)
                acc[here, :] += jnp.dot(
                    root_all[source, here, columns], panel_all[origin],
                    preferred_element_type=jnp.float32,
                )

    def arrive_root(event):
        step, way, chunk = event
        origin = sub_at(chip + sign[way] * step, core)
        wait_root(event, origin)
        send_root((step + 1, way, chunk))
        if step == 1 and first_sends.index(event) + IN_FLIGHT < len(first_sends):
            send_root(first_sends[first_sends.index(event) + IN_FLIGHT])
        forward = twin_copy(step, way, chunk, origin)
        forward.start()
        sends.append(forward)

    def wait_root(event, origin):
        step, way, chunk = event
        region = root_all.at[origin, pl.ds(chunk * root_rows, root_rows)]
        pltpu.make_async_remote_copy(
            src_ref=region, dst_ref=region,
            send_sem=root_send.at[way, step - 1, chunk],
            recv_sem=root_recv.at[way, step - 1, chunk],
            device_id={"sub": sub_at(chip - sign[way], core)}, device_id_type=MESH,
        ).wait_recv()

    def arrive_panel(event):
        step, way, chunk = event
        panel_copy(step, way, chunk, blk_at(place + sign[way] * step)).wait_recv()
        send_panel((step + 1, way, chunk))

    merged = []
    for at, event in enumerate(panel_events):
        merged.append((0.87 * (at + 1) / len(panel_events), 0, event))
    for at, event in enumerate(root_events[:-2]):
        merged.append(((at + 1) / len(root_events), 1, event))
    merged.sort()

    contract_rows = (((0,), (0,)), ((), ()))
    inverse_fetch.wait()
    square[...] = lax.dot_general(
        inverse_own[...], inverse_own[...], contract_rows, preferred_element_type=jnp.float32
    )
    local.wait()
    pltpu.make_async_remote_copy(
        src_ref=root_ref, dst_ref=root_all.at[twin], send_sem=own_twin_send, recv_sem=own_twin_recv,
        device_id={"sub": twin}, device_id_type=MESH,
    ).wait_recv()
    near_dot(blk)
    for _, kind, event in merged:
        if kind == 1:
            arrive_root(event)
            continue
        arrive_panel(event)
        step, way, chunk = event
        if chunk == PANEL_CHUNKS - 1:
            if step == half:
                near_dot(blk_at(place + half))
            else:
                near_dot(blk_at(place + sign[way] * step))

    last = chips // 2

    def far_dot(events):
        step, way, chunk = events[0]
        origin = sub_at(chip + sign[way] * step, core)
        other = sub_at(chip + sign[way] * step, 1 - core)
        for event in events:
            twin_copy(*event, other).wait_recv()
        here = pl.ds(chunk * root_rows, len(events) * root_rows)
        total = acc[here, :]
        for source in (origin, other):
            for at in range(ratio):
                total += jnp.dot(
                    root_all[source, here, at * rows:(at + 1) * rows], panel_all[source * ratio + at],
                    preferred_element_type=jnp.float32,
                )
        if step < last:
            acc[here, :] = total
            return
        rounded = total.astype(jnp.bfloat16)
        keep = keeps[chunk * root_rows // piece_rows]
        cross_ref[here, :] = jnp.where(keep, -rounded, jnp.zeros_like(rounded))
        square[...] += lax.dot_general(
            panel_all[blk, here, :], rounded, contract_rows, preferred_element_type=jnp.float32
        )

    for step in range(1, last + 1):
        for way in (0, 1):
            chunks = [event for event in root_events if event[:2] == (step, way)]
            for at in range(0, len(chunks), 2):
                if (step, way, chunks[at][2]) == (last, 1, ROOT_CHUNKS - 2):
                    for event in root_events[-2:]:
                        arrive_root(event)
                        far_dot([event])
                else:
                    far_dot(chunks[at:at + 2])

    part[...] = square[...].astype(jnp.bfloat16).reshape(blks, owned, width)
    for offset in range(1, blks):
        target = lax.rem(blk + offset, blks)
        copy = pltpu.make_async_remote_copy(
            src_ref=part.at[target], dst_ref=got.at[offset - 1],
            send_sem=part_send.at[offset - 1], recv_sem=part_recv.at[offset - 1],
            device_id={"blk": target}, device_id_type=MESH,
        )
        copy.start()
        sends.append(copy)
    total = part[blk].astype(jnp.float32)
    for offset in range(1, blks):
        sends[offset - blks].wait_recv()
        total += got[offset - 1].astype(jnp.float32)
    rows_at = blk * owned + lax.broadcasted_iota(jnp.int32, (owned, width), 0)
    cols_at = lax.broadcasted_iota(jnp.int32, (owned, width), 1)
    diag_ref[...] = jnp.where(cols_at <= rows_at, total, jnp.zeros_like(total))
    for copy in sends:
        copy.wait_send()


def local(subs, blks, root_inverse, factor_panel, diag_inverse, pattern):
    rows, width = factor_panel.shape
    cols = root_inverse.shape[1]
    owned = diag_inverse.shape[0]
    dma = pltpu.SemaphoreType.DMA
    panel_sems = dma((2, blks // 2, PANEL_CHUNKS))
    root_sems = dma((2, subs // 4, ROOT_CHUNKS))
    hbm = pl.BlockSpec(memory_space=pl.ANY)
    vmem = pl.BlockSpec(memory_space=pltpu.VMEM)
    return pl.pallas_call(
        functools.partial(kernel, subs, blks),
        out_shape=(
            jax.ShapeDtypeStruct((rows, width), jnp.bfloat16),
            jax.ShapeDtypeStruct((owned, width), jnp.float32),
        ),
        in_specs=[
            pl.BlockSpec(memory_space=pltpu.SMEM), hbm, hbm, hbm,
        ],
        out_specs=(vmem, vmem),
        scratch_shapes=[
            pltpu.VMEM((subs, rows, cols), jnp.bfloat16),
            pltpu.VMEM((blks, rows, width), jnp.bfloat16),
            pltpu.VMEM((rows, width), jnp.float32),
            pltpu.VMEM((rows, width), jnp.bfloat16),
            pltpu.VMEM((owned, width), jnp.bfloat16),
            pltpu.VMEM((width, width), jnp.float32),
            pltpu.VMEM((blks, owned, width), jnp.bfloat16),
            pltpu.VMEM((blks - 1, owned, width), jnp.bfloat16),
            dma(()), dma(()), dma(()), panel_sems, panel_sems, root_sems, root_sems, root_sems, root_sems, dma(()), dma(()),
            dma((blks - 1,)), dma((blks - 1,)),
        ],
        compiler_params=pltpu.CompilerParams(
            collective_id=0, has_side_effects=True, vmem_limit_bytes=60 * 1024 * 1024
        ),
    )(pattern, root_inverse, factor_panel, diag_inverse)


SUB = 2
TILE = 256
(
    TWIN, LIFT, UPDOWN, ACROSS, VIA, HOP, HOP_SIDE_A, HOP_UP_A, HOP_UP_B, LIFT_A, SIDE_A, HOP_SIDE_B, LIFT_B, DROP, TOP,
    LIFT_SIDE, VIA_HOP, TOP_SIDE, BACK_A, BACK_B, SUM_SIDE, SUM_B, SUM_A, SUM_HOME, PAIR,
) = range(25)
COL, OUTER, INNER, FINISH, BEGIN = range(5)
STEPS = (
    (BEGIN, 0), (COL, 0), (COL, 1), (COL, 2), (COL, 3), (OUTER, 0), (INNER, 0), (OUTER, 1), (INNER, 1), (FINISH, 0),
    (OUTER, 2), (INNER, 2), (FINISH, 1), (OUTER, 3), (INNER, 3), (FINISH, 2), (FINISH, 3),
)
PROGRAMS = (
    (
        200, 201, 300, 301, 30400, 10500, 20300, 600, 20200, 210, 10501, 20301, 601, 20201, 211, 20210, 700,
        20600, 310, 20211, 701, 10510, 20601, 610, 10600, 10601, 30100, 1800, 1801, 10300, 10301, 30200, 10511,
        20310, 611, 20700, 710, 20701, 800, 20710, 801, 10520, 20610, 620, 20800, 711, 10610, 20801, 810,
        10521, 20611, 621, 10611, 20711, 811, 20620, 311, 30110, 21800, 1810, 21801, 1811, 10310, 10311, 30210,
        12400, 12401, 12300, 12301, 30300, 10530, 20621, 630, 10620, 20810, 820, 10531, 20311, 631, 20811, 720,
        10621, 30120, 21810, 1820, 20820, 821, 21811, 1821, 20720, 721, 10630, 20821, 830, 20721, 730, 10631,
        20830, 831, 20730, 731, 10320, 10321, 10020, 10021, 30220, 2420, 2421, 12410, 12411, 12310, 12311,
        30310, 30130, 21820, 1830, 21821, 1831, 10330, 10331, 10030, 10031, 30230, 2430, 2431,
    ),
    (
        20, 21, 30400, 11600, 600, 11601, 601, 30, 31, 220, 221, 11610, 20600, 610, 11620, 20601, 620, 20220,
        230, 10600, 10601, 30100, 1900, 1901, 10200, 10201, 11300, 11301, 30200, 2400, 2401, 11611, 20610, 611,
        11621, 20620, 621, 20221, 231, 10610, 10611, 30110, 21900, 1910, 21901, 1911, 10210, 10211, 11310,
        11311, 30210, 11630, 20611, 630, 20621, 320, 11631, 20630, 631, 20320, 321, 2410, 2411, 10620, 10621,
        30120, 21910, 1920, 21911, 1921, 10220, 10221, 11320, 11321, 30220, 20631, 330, 20321, 331, 10630,
        10631, 30130, 21920, 1930, 21921, 1931, 10230, 10231, 11330, 11331, 30230, 12420, 12421, 12320, 12321,
        30320, 12430, 12431, 12330, 12331, 30330,
    ),
    (
        100, 101, 30400, 210, 211, 300, 301, 20300, 310, 10200, 20100, 900, 10201, 20101, 901, 0, 1, 10, 11,
        20301, 311, 10210, 20900, 910, 20901, 110, 20310, 1000, 20311, 1001, 10211, 20910, 911, 20210, 200,
        20211, 201, 10220, 20110, 920, 20911, 111, 21000, 1010, 21001, 1011, 10221, 20920, 921, 10700, 10701,
        10800, 10801, 30100, 1800, 1801, 11000, 11001, 30200, 21010, 1020, 21011, 1021, 10230, 20111, 930,
        10231, 20921, 931, 10710, 10711, 10810, 10811, 30110, 21800, 1810, 21801, 1811, 11010, 11011, 30210,
        12400, 12401, 12300, 12301, 30300, 10720, 10721, 10820, 10821, 30120, 21810, 1820, 21811, 1821, 21020,
        1030, 21021, 1031, 11020, 11021, 30220, 2420, 2421, 12410, 12411, 12310, 12311, 30310, 10730, 10731,
        10830, 10831, 30130, 21820, 1830, 21821, 1831, 11030, 11031, 30230, 2430, 2431,
    ),
    (
        30400, 10300, 1300, 10301, 1301, 10500, 1100, 10501, 1101, 21300, 220, 10510, 21100, 1110, 21301, 221,
        10511, 21101, 1111, 10310, 20220, 1310, 11100, 11101, 30100, 1900, 1901, 1200, 120, 21200, 1201, 10520,
        21110, 1120, 20120, 121, 10311, 20221, 1311, 21111, 320, 10000, 10001, 30200, 2400, 2401, 11110, 11111,
        30110, 21900, 1910, 21901, 1911, 10521, 21120, 1121, 21310, 230, 21201, 1210, 20320, 321, 21311, 231,
        20121, 1211, 21121, 330, 10320, 20230, 1320, 10010, 10011, 30210, 2410, 2411, 11120, 11121, 30120,
        21910, 1920, 21911, 1921, 10321, 30220, 20231, 1321, 20321, 331, 21210, 130, 21211, 1220, 10530, 20330,
        1130, 20130, 1221, 21220, 131, 10330, 21320, 1330, 10531, 20331, 1131, 10331, 21321, 1331, 11130,
        11131, 30130, 21920, 1930, 21921, 1931, 21221, 1230, 30230, 12420, 12421, 12320, 12321, 30320, 20131,
        1231, 12430, 12431, 12330, 12331, 30330,
    ),
    (
        0, 1, 500, 30400, 10, 11, 501, 400, 401, 30000, 2000, 2001, 30010, 20400, 410, 20401, 411, 20500, 510,
        10020, 10021, 30020, 22000, 2010, 20501, 511, 10900, 20410, 1400, 10901, 20411, 1401, 10030, 10031,
        30030, 22001, 2011, 22010, 1500, 22011, 1501, 12200, 12000, 2300, 10910, 21500, 1510, 12201, 12001,
        2301, 21400, 1410, 10911, 21501, 1511, 21510, 2020, 21401, 1411, 21511, 2021, 10920, 21410, 1420,
        12210, 12010, 22300, 2310, 22020, 1520, 11500, 11501, 30200, 12211, 12011, 22301, 2311, 10921, 21411,
        1421, 22021, 2030, 21520, 1521, 12220, 12020, 22310, 2320, 22030, 2031, 12221, 12021, 22311, 2321,
        10930, 21420, 1430, 11510, 11511, 30210, 12400, 12401, 11800, 11801, 11900, 11901, 30300, 11520, 11521,
        30220, 12410, 12411, 11810, 11811, 11910, 11911, 30310, 10931, 21421, 1431, 21521, 1530, 12230, 12030,
        22320, 2330, 22031, 1531, 12231, 12031, 22321, 2331, 11530, 11531, 30230, 2430, 2431, 2420, 2421,
    ),
    (
        30400, 10000, 10001, 30000, 20, 21, 520, 521, 12100, 2000, 12101, 2001, 10100, 1400, 10101, 1401, 30,
        31, 20520, 530, 20521, 531, 10010, 10011, 30010, 30020, 30030, 21400, 420, 21401, 421, 12200, 12000,
        2300, 12110, 22000, 2010, 20420, 430, 10110, 20421, 1410, 12201, 12001, 2301, 12111, 22001, 2011,
        20430, 431, 12210, 12010, 22300, 2310, 12120, 22010, 2020, 10111, 21410, 1411, 12211, 12011, 22301,
        2311, 12121, 22011, 2021, 10120, 20431, 1420, 11200, 11201, 30200, 2400, 2401, 10121, 21411, 1421,
        11210, 11211, 30210, 12220, 12020, 22310, 2320, 2410, 2411, 10130, 21420, 1430, 12221, 12021, 22311,
        2321, 12130, 22020, 2030, 10131, 21421, 1431, 12131, 22021, 2031, 12230, 12030, 22320, 2330, 12231,
        12031, 22321, 2331, 11220, 11221, 30220, 11230, 11231, 30230, 12420, 12421, 11820, 11821, 11920, 11921,
        30320, 12430, 12431, 11830, 11831, 11930, 11931, 30330,
    ),
    (
        0, 1, 30400, 10, 11, 500, 30000, 2000, 501, 2001, 20500, 510, 30010, 10400, 20501, 1600, 22000, 2010,
        10401, 20510, 1601, 22001, 2011, 10020, 10021, 30020, 21600, 511, 10030, 10031, 30030, 22010, 2030,
        12000, 2200, 22011, 2020, 10410, 21601, 1610, 22030, 2021, 22020, 2031, 10411, 20511, 1611, 12001,
        2201, 11400, 22021, 1700, 11401, 22031, 1701, 12010, 22200, 2210, 12011, 22201, 2211, 11700, 11701,
        30200, 11410, 21700, 1710, 11411, 21701, 1711, 12020, 22210, 2220, 12021, 22211, 2221, 11420, 21710,
        1720, 11710, 11711, 30210, 12400, 12401, 11800, 11801, 11900, 11901, 30300, 12030, 22220, 2230, 11421,
        21711, 1721, 11430, 21720, 1730, 12031, 22221, 2231, 11431, 21721, 1731, 11720, 11721, 30220, 2420,
        2421, 12410, 12411, 11810, 11811, 11910, 11911, 30310, 11730, 11731, 30230, 2430, 2431,
    ),
    (
        20, 21, 30400, 10000, 10001, 30000, 2100, 2101, 10010, 10011, 30010, 30020, 30, 31, 22100, 2200, 30030,
        22101, 2110, 22200, 2201, 22110, 2111, 520, 521, 22201, 2210, 11400, 1700, 10420, 20520, 1620, 11401,
        1701, 10421, 20521, 1621, 22111, 2211, 22210, 2120, 21620, 530, 11700, 11701, 30200, 22211, 2121, 2400,
        2401, 22120, 2220, 21621, 531, 11410, 21700, 1710, 10430, 20530, 1630, 22121, 2221, 10431, 20531, 1631,
        11411, 21701, 1711, 22220, 2130, 11420, 21710, 1720, 22221, 2230, 22130, 2131, 11421, 21711, 1721,
        22230, 2231, 11430, 21720, 1730, 11710, 11711, 30210, 2410, 2411, 11720, 11721, 30220, 11431, 21721,
        1731, 11730, 11731, 30230, 12420, 12421, 11820, 11821, 11920, 11921, 30320, 12430, 12431, 11830, 11831,
        11930, 11931, 30330,
    ),
)
ROWS = (((0,), (0,)), ((), ()))


def plane_kernel(
    pattern_ref, root_ref, panel_ref, inverse_ref, cross_ref, diag_ref,
    root, panel, inverse, cross, own, gathered, mine, relay, acc, staged, twin_in, outer, outer_in, col, col_in,
    square, part, got, root_sem, panel_sem, inverse_sem, cross_sem, send_sem, recv_sem, part_send, part_recv,
):
    rows, width = panel_ref.shape
    half = width // 2
    owned = diag_ref.shape[0]
    blks = width // owned
    tile = min(rows, TILE)
    piece = rows // SUB
    sub, blk = lax.axis_index("sub"), lax.axis_index("blk")
    x, core_at, z_at, y = sub // 2, sub % 2, blk // 2, blk % 2
    level = z_at + x * (3 - 2 * z_at)
    core = core_at + x * (1 - 2 * core_at)

    def device(level_to, y_to, core_to, plane):
        return {
            "sub": plane * 2 + core_to + plane * (1 - 2 * core_to),
            "blk": (level_to + plane * (3 - 2 * level_to)) * 2 + y_to,
        }

    def here(level_to, y_to, core_to):
        return device(level_to, y_to, core_to, x)

    def there(level_to, y_to, core_to):
        return device(level_to, y_to, core_to, 1 - x)

    def twin():
        return {"sub": x * 2 + 1 - core_at}


    barrier = pltpu.get_barrier_semaphore()
    for offset in range(1, 2 * blks):
        other = lax.rem(core_at * blks + blk + offset, 2 * blks)
        pl.semaphore_signal(
            barrier, inc=1, device_id={"sub": x * 2 + other // blks, "blk": other % blks}, device_id_type=MESH
        )
    for offset in range(2):
        pl.semaphore_signal(barrier, inc=1, device_id={"sub": (1 - x) * 2 + offset}, device_id_type=MESH)

    def halves(ref, h):
        return ref.at[:, pl.ds(h * half, half)]

    panel_fetch = pltpu.make_async_copy(panel_ref, panel, panel_sem)
    panel_fetch.start()
    root_fetch = pltpu.make_async_copy(root_ref, root, root_sem)
    root_fetch.start()
    inverse_fetch = pltpu.make_async_copy(inverse_ref, inverse, inverse_sem)
    inverse_fetch.start()

    def at(level_of, core_of, body):
        pl.when((level == level_of) & (core == core_of))(body)

    def cut(s):
        return pl.ds(s * piece, piece)

    def copy(kind, j, s, source, target, to):
        return pltpu.make_async_remote_copy(
            src_ref=source, dst_ref=target, send_sem=send_sem.at[kind, j, s], recv_sem=recv_sem.at[kind, j, s],
            device_id=to, device_id_type=MESH,
        )

    def outgoing(level_of, core_of, kind, j, s):
        g, h = j // 2, j % 2
        far = 1 - y
        given = own.at[h, cut(s)]
        inner_near, inner_far = gathered.at[0, j, y, cut(s)], gathered.at[0, j, far, cut(s)]
        outer_near, outer_far = gathered.at[1, j, y, cut(s)], gathered.at[1, j, far, cut(s)]
        via = relay.at[h, cut(s)]
        sum_near, sum_far = col.at[j, y, cut(s)], col.at[j, far, cut(s)]
        source, target, to = {
            TWIN: lambda: (given, inner_near if level_of < 2 else mine.at[j, cut(s)], twin()),
            LIFT: lambda: (given, inner_near, here(2, y, 1)),
            UPDOWN: lambda: (given, inner_near, here(1 - level_of, y, level_of)),
            ACROSS: lambda: (given, inner_near, here(level_of, far, level_of)),
            VIA: lambda: (given, via, here(3, y, g)),
            HOP: lambda: (given, outer_near, there(3 - level_of, y, 3 - level_of)),
            HOP_SIDE_A: lambda: (outer_near, outer_near, here(0, far, core_of)),
            HOP_UP_A: lambda: (outer_near, outer_near, here(1, y, 0)),
            HOP_UP_B: lambda: (outer_far, outer_far, here(1, y, 0)),
            LIFT_A: lambda: (inner_near, inner_near, here(2, y, 0)),
            SIDE_A: lambda: (inner_near, inner_near, here(1, far, 0)),
            HOP_SIDE_B: lambda: (outer_near, outer_near, here(1, far, 1)),
            LIFT_B: lambda: (inner_far, inner_far, here(2, y, 1)),
            DROP: lambda: (inner_far, inner_far, here(0, y, 1)),
            TOP: lambda: (inner_near, inner_near, here(3, y, core_of)),
            LIFT_SIDE: lambda: (inner_near, inner_near, here(2, far, 0)),
            VIA_HOP: lambda: (via, outer_near, there(0, y, 1)),
            TOP_SIDE: lambda: (inner_near, inner_near, here(3, far, core_of)),
            BACK_A: lambda: (outer.at[j, cut(s)], outer_in.at[0, h, cut(s)], there(3 - level_of, y, g)),
            BACK_B: lambda: (outer.at[j, cut(s)], outer_in.at[1, h, cut(s)], there(3 - level_of, y, g)),
            SUM_SIDE: lambda: (sum_far, col_in.at[0, j, cut(s)], here(level_of, far, core_of)),
            SUM_B: lambda: (sum_far, col_in.at[2, j, cut(s)], here(2, y, 1)),
            SUM_A: lambda: (sum_near, col_in.at[1, j, cut(s)], here(2, y, core_of)),
            SUM_HOME: lambda: (sum_near, outer_in.at[0, h, cut(s)], here(core_of, y, g)),
            PAIR: lambda: (staged.at[j, cut(s)], twin_in.at[h, cut(s)], twin()),
        }[kind]()
        return copy(kind, j, s, source, target, to)

    def incoming(level_of, kind, j, s):
        h = j % 2
        if kind == TWIN and level_of >= 2:
            region = mine.at[j, cut(s)]
        elif kind in (TWIN, LIFT, UPDOWN, LIFT_A, TOP):
            region = gathered.at[0, j, y, cut(s)]
        elif kind in (ACROSS, SIDE_A, LIFT_SIDE, TOP_SIDE, LIFT_B, DROP):
            region = gathered.at[0, j, 1 - y, cut(s)]
        elif kind in (HOP, HOP_UP_A, VIA_HOP):
            region = gathered.at[1, j, y, cut(s)]
        elif kind in (HOP_SIDE_A, HOP_SIDE_B, HOP_UP_B):
            region = gathered.at[1, j, 1 - y, cut(s)]
        elif kind == VIA:
            region = relay.at[h, cut(s)]
        elif kind in (SUM_SIDE, SUM_A, SUM_B):
            region = col_in.at[(SUM_SIDE, SUM_A, SUM_B).index(kind), j, cut(s)]
        elif kind in (BACK_A, BACK_B):
            region = outer_in.at[kind - BACK_A, h, cut(s)]
        else:
            region = (outer_in.at[0, h, cut(s)] if kind == SUM_HOME else twin_in.at[h, cut(s)])
        return copy(kind, j, s, region, region, twin())

    def add_in(j, s, y_of, slots):
        total = col[j, y_of, cut(s)].astype(jnp.float32)
        for slot in slots:
            total += col_in[slot, j, cut(s)].astype(jnp.float32)
        col[j, y_of, cut(s)] = total.astype(jnp.bfloat16)

    def act(level_of, core_of, code):
        op, kind, j, s = code // 10000, code // 100 % 100, code // 10 % 10, code % 10
        if op == 1:
            incoming(level_of, kind, j, s).wait_recv()
        elif op == 2:
            outgoing(level_of, core_of, kind, j, s).wait_send()
        else:
            if (kind, level_of, core_of) == (SUM_A, 3, 0):
                add_in(j, s, y, (0,))
            if (kind, level_of, core_of) == (SUM_SIDE, 2, 1):
                add_in(j, s, 1 - y, (2,))
            if kind == SUM_HOME:
                add_in(j, s, y, (0, 1))
            outgoing(level_of, core_of, kind, j, s).start()

    at_code = [0] * len(PROGRAMS)

    def links(step):
        for n, program in enumerate(PROGRAMS):
            start = at_code[n]
            if step is None:
                end = len(program)
            elif step in program:
                end = program.index(step)
                at_code[n] = end + 1
            else:
                continue
            codes = program[start:end]
            if step is None:
                sent = {code for code in program if code < 10000}
                codes += tuple(sorted(20000 + code for code in sent if 20000 + code not in program))

            def body(level_of=n // 2, core_of=n % 2, codes=codes):
                for code in codes:
                    act(level_of, core_of, code)
            if codes:
                at(n // 2, n % 2, body)

    def times(q, j, at_row):
        span = pl.ds(at_row, tile)
        return jnp.dot(
            root[span, :rows], gathered[q, j, 0], preferred_element_type=jnp.float32
        ) + jnp.dot(root[span, rows:], gathered[q, j, 1], preferred_element_type=jnp.float32)

    def over_rows(body):
        @pl.loop(0, rows // tile)
        def _(step):
            body(pl.multiple_of(step * tile, tile))

    def outer_work(j):
        @pl.when(level < 2)
        def _():
            def body(at_row):
                outer[j, pl.ds(at_row, tile)] = times(1, j, at_row).astype(jnp.bfloat16)
            over_rows(body)

    def col_work(j):
        @pl.when(level >= 2)
        def _():
            for y_of in range(2):
                def body(at_row):
                    columns = pl.ds(y_of * rows + at_row, tile)
                    col[j, y_of, pl.ds(at_row, tile)] = lax.dot_general(
                        root[:, columns], mine[j], ROWS, preferred_element_type=jnp.float32
                    ).astype(jnp.bfloat16)
                over_rows(body)

    def inner_work(j):
        def body(at_row):
            span = pl.ds(at_row, tile)
            value = times(0, j, at_row)
            acc[j, span] = value
            staged[j, span] = value.astype(jnp.bfloat16)
        over_rows(body)

    keep_rows = min(rows, BLOCK)

    def finish(j):
        g, h = j // 2, j % 2

        @pl.when(core == g)
        def _():
            @pl.when(level < 2)
            def _():
                def body(at_row):
                    span = pl.ds(at_row, tile)
                    acc[j, span] += outer_in[0, h, span].astype(jnp.float32)
                over_rows(body)

            @pl.when(level >= 2)
            def _():
                def body(at_row):
                    span = pl.ds(at_row, tile)
                    acc[j, span] += outer_in[0, h, span].astype(jnp.float32) + outer_in[1, h, span].astype(jnp.float32)
                over_rows(body)

            for step in range(rows // tile):
                span = pl.ds(step * tile, tile)
                rounded = (acc[j, span] + twin_in[h, span].astype(jnp.float32)).astype(jnp.bfloat16)
                keep = keeps[step * tile // keep_rows]
                cross[h, span] = jnp.where(keep, -rounded, jnp.zeros_like(rounded))
                for a in range(h, 2):
                    square[a * half:(a + 1) * half, h * half:(h + 1) * half] += lax.dot_general(
                        own[a, span], rounded, ROWS, preferred_element_type=jnp.float32
                    )

    def cross_store(h):
        return pltpu.make_async_copy(cross.at[h], halves(cross_ref, h), cross_sem.at[h])

    def first_owner(h):
        return h * (blks // 2)

    def wide(h, owner):
        lanes = min(half, 128)
        return min(half, -((h * half - (owner + 1) * owned) // lanes) * lanes)

    def part_copy(h, sender, owner, to):
        columns = pl.ds(0, wide(h, owner))
        return pltpu.make_async_remote_copy(
            src_ref=part.at[h, owner, :, columns], dst_ref=got.at[h, sender, :, columns],
            send_sem=part_send.at[h, owner], recv_sem=part_recv.at[h, sender],
            device_id={"blk": to}, device_id_type=MESH,
        )

    def part_sends(j):
        h = j % 2

        @pl.when(core == j // 2)
        def _():
            first = first_owner(h)
            lower = square[first * owned:, h * half:(h + 1) * half]
            part[h, first:] = lower.astype(jnp.bfloat16).reshape(blks - first, owned, half)
            for owner in reversed(range(first, blks)):
                @pl.when(owner != blk)
                def _():
                    part_copy(h, blk, owner, owner).start()
            cross_store(h).start()

    def part_sum(h, owner):
        @pl.when(blk == owner)
        def _():
            columns = wide(h, owner)
            total = part[h, owner, :, :columns].astype(jnp.float32)
            for sender in range(blks):
                if sender != owner:
                    part_copy(h, sender, owner, sender).wait_recv()
                    total += got[h, sender, :, :columns].astype(jnp.float32)
            rows_at = owner * owned + lax.broadcasted_iota(jnp.int32, (owned, columns), 0)
            cols_at = h * half + lax.broadcasted_iota(jnp.int32, (owned, columns), 1)
            diag_ref[:, h * half:h * half + columns] = jnp.where(cols_at <= rows_at, total, jnp.zeros_like(total))

    keeps = [pattern_ref[0, (blk * rows + step * keep_rows) // BLOCK] > 0 for step in range(rows // keep_rows)]

    def mask(h):
        for step, keep in enumerate(keeps):
            span = pl.ds(step * keep_rows, keep_rows)
            values = panel[span, h * half:(h + 1) * half]
            values = jnp.where(keep, values, jnp.zeros_like(values))
            own[h, span] = values

            @pl.when(level >= 2)
            def _():
                mine[2 * core + h, span] = values

            @pl.when(level == core)
            def _():
                gathered[0, 2 * core + h, y, span] = values

    def begin(_):
        mask(1)
        inverse_fetch.wait()
        square[...] = lax.dot_general(inverse[...], inverse[...], ROWS, preferred_element_type=jnp.float32)
        diag_ref[...] = jnp.zeros_like(diag_ref)
        root_fetch.wait()

    panel_fetch.wait()
    mask(0)
    pl.semaphore_wait(barrier, 2 * blks + 1)
    for kind, j in STEPS:
        links(30000 + kind * 100 + j * 10)
        (col_work, outer_work, inner_work, finish, begin)[kind](j)
        if kind == FINISH:
            part_sends(j)
    for h in range(2):
        for owner in range(first_owner(h), blks):
            part_sum(h, owner)
    links(None)
    for h in range(2):
        cross_store(h).wait()
        for owner in range(first_owner(h), blks):
            @pl.when(blk != owner)
            def _():
                part_copy(h, blk, owner, owner).wait_send()


def hand_on(cross_in, diag_in, cross_out, diag_out):
    cross_out[...] = cross_in[...]
    diag_out[...] = diag_in[...]


def plane_local(blks, root_inverse, factor_panel, diag_inverse, pattern):
    rows, width = factor_panel.shape
    half = width // 2
    owned = diag_inverse.shape[0]
    dma = pltpu.SemaphoreType.DMA
    hbm = pl.BlockSpec(memory_space=pl.ANY)
    vmem = pl.BlockSpec(memory_space=pltpu.VMEM)

    def held(*lead, dtype=jnp.bfloat16):
        return pltpu.VMEM((*lead, rows, half), dtype)

    cross, diag = pl.pallas_call(
        plane_kernel,
        out_shape=(
            jax.ShapeDtypeStruct((rows, width), jnp.bfloat16),
            jax.ShapeDtypeStruct((owned, width), jnp.float32),
        ),
        in_specs=[pl.BlockSpec(memory_space=pltpu.SMEM), hbm, hbm, hbm],
        out_specs=(hbm, vmem),
        scratch_shapes=[
            pltpu.VMEM(root_inverse.shape, jnp.bfloat16),
            pltpu.VMEM((rows, width), jnp.bfloat16),
            pltpu.VMEM((owned, width), jnp.bfloat16),
            held(2), held(2), held(2, 4, 2), held(4), held(2), held(4, dtype=jnp.float32), held(4), held(2),
            held(4), held(2, 2), held(4, 2), held(3, 4),
            pltpu.VMEM((width, width), jnp.float32),
            pltpu.VMEM((2, blks, owned, half), jnp.bfloat16),
            pltpu.VMEM((2, blks, owned, half), jnp.bfloat16),
            dma(()), dma(()), dma(()), dma((2,)), dma((25, 4, SUB)), dma((25, 4, SUB)), dma((2, blks)), dma((2, blks)),
        ],
        compiler_params=pltpu.CompilerParams(
            collective_id=1, has_side_effects=True, vmem_limit_bytes=60 * 1024 * 1024
        ),
    )(pattern, root_inverse, factor_panel, diag_inverse)
    return pl.pallas_call(
        hand_on,
        out_shape=(jax.ShapeDtypeStruct(cross.shape, cross.dtype), jax.ShapeDtypeStruct(diag.shape, diag.dtype)),
        in_specs=[vmem, vmem],
        out_specs=(vmem, vmem),
    )(cross, diag)


def fits(mesh, root_inverse, factor_panel):
    subs, blks = mesh.shape["sub"], mesh.shape["blk"]
    rows, columns = root_inverse.shape
    return (subs, blks) == (4, 8) and factor_panel.shape[1] % (4 * 256) == 0 and rows % (blks * BLOCK) == 0


def solution(mesh):
    subs, blks = mesh.shape["sub"], mesh.shape["blk"]

    def run(root_inverse, factor_panel, diag_inverse, pattern):
        body = functools.partial(local, subs, blks)
        if fits(mesh, root_inverse, factor_panel):
            body = functools.partial(plane_local, blks)
        return jax.shard_map(
            body,
            mesh=mesh,
            in_specs=(P("blk", "sub"), P("blk", "sub"), P("blk", "sub"), P("sub", None)),
            out_specs=(P("blk", "sub"), P("blk", "sub")),
            check_vma=False,
        )(root_inverse, factor_panel, diag_inverse, pattern)

    return run
```
